512 devices in a mesh: dp: 64 (over z, y_hi, x), mp: 8 (over y_lo, core).
Axes of the slice: x: 4, y: 8 (y_hi: 2, y_lo: 4; y = y_hi * 4 + y_lo), z: 8, core: 2. Of those that a mesh axis runs over, the one named last changes fastest.
Arguments:
- tokens: bfloat16 [32768, 8192], P('dp', 'mp'), may hold values from -6 to 6
- upstream: bfloat16 [32768, 8192], P('dp', 'mp'), may hold values from -6 to 6
- first_factor: bfloat16 [32, 256, 256], P('mp', 'dp'), may hold values from -0.375 to 0.375
- second_factor: bfloat16 [32, 256, 256], P('mp', 'dp'), may hold values from -0.375 to 0.375
Outputs:
- mixed: bfloat16 [32768, 8192], P('dp', 'mp')
- grad_tokens: bfloat16 [32768, 8192], P('dp', 'mp')
- grad_first: float32 [32, 256, 256], P('mp', 'dp')
- grad_second: float32 [32, 256, 256], P('mp', 'dp')
The draws below stay inside these ranges and needn't reach their ends.
All inputs are finite; a program needn't handle non-finite values.
Results may differ from the reference program's by a relative error of at most 0.0056.
Values may be sent and summed in bfloat16 or wider, within the bound.
A program may use at most 64 MiB of HBM per device.

```python
import math
import jax
import jax.numpy as jnp
from jax import lax

BLOCKS = 32
BLK = 256
TOK_DEV = 512
D = 8192
TOKENS = 32768


def shard_levels(own_key, shape, cuts, smallest, largest):
    def one(axis_at, shards_of):
        draws = jax.random.uniform(jax.random.fold_in(jax.random.fold_in(own_key, 6), axis_at), (shards_of,), jnp.float32, smallest / len(cuts), largest / len(cuts))
        return jnp.repeat(jnp.exp(draws), shape[axis_at] // shards_of).reshape((-1,) + (1,) * (len(shape) - axis_at - 1))

    factor_of = one(*cuts[0])
    for cut in cuts[1:]:
        factor_of = factor_of * one(*cut)
    return factor_of


def noise(stream_key, extent, deviation, limit, cuts=(), kind=jnp.bfloat16):
    values = deviation * jax.random.normal(stream_key, extent, jnp.float32)
    if cuts:
        values = values * shard_levels(stream_key, extent, cuts, -0.22, 0.18)
    return jnp.clip(values, -limit, limit).astype(kind)


def setup_inputs(seed: int = 0) -> dict:
    key_list = jax.random.split(jax.random.key(seed), 5)
    tokens = noise(key_list[0], (TOKENS, D), 1.0, 6.0, ((0, 64), (1, 8)))
    upstream = noise(key_list[1], (TOKENS, D), 1.0, 6.0, ((0, 64), (1, 8)))
    first_factor = noise(key_list[2], (BLOCKS, BLK, BLK), BLK ** -0.5, 0.375, ((0, 8), (1, 64)))
    second_factor = noise(key_list[3], (BLOCKS, BLK, BLK), BLK ** -0.5, 0.375, ((0, 8), (1, 64)))
    return {"tokens": tokens, "upstream": upstream, "first_factor": first_factor, "second_factor": second_factor}


def gelu_exact(value):
    return jax.nn.gelu(value, approximate=False)

def reference(tokens, upstream, first_factor, second_factor):
    left_blocks = first_factor.astype(jnp.float32)
    right_blocks = second_factor.astype(jnp.float32)

    def block_step(carry, paired):
        grad_left, grad_right = carry
        row_block, cotangent = paired
        tok_count = row_block.shape[0]
        shaped = row_block.reshape(tok_count, BLOCKS, BLK).astype(jnp.float32)
        first_out = jnp.einsum('tbi,bio->tbo', shaped, left_blocks).astype(jnp.bfloat16)
        moved_in = jnp.transpose(first_out, (0, 2, 1)).reshape(tok_count, BLOCKS, BLK).astype(jnp.float32)
        second_out = jnp.einsum('tjc,jck->tjk', moved_in, right_blocks)
        activated, pullback = jax.vjp(gelu_exact, second_out)
        mixed_rows = (row_block.astype(jnp.float32) + activated.reshape(tok_count, D)).astype(jnp.bfloat16)
        upstream_rows = cotangent.astype(jnp.float32)
        grad_out = pullback(upstream_rows.reshape(tok_count, BLOCKS, BLK))[0].astype(jnp.bfloat16)
        grad_out = lax.optimization_barrier(grad_out).astype(jnp.float32)
        grad_right = grad_right + jnp.einsum('tjc,tjk->jck', moved_in, grad_out)
        grad_moved = jnp.einsum('tjk,jck->tjc', grad_out, right_blocks).astype(jnp.bfloat16)
        grad_moved = lax.optimization_barrier(grad_moved)
        grad_inner = jnp.transpose(grad_moved.reshape(tok_count, BLK, BLOCKS), (0, 2, 1)).astype(jnp.float32)
        grad_left = grad_left + jnp.einsum('tbi,tbo->bio', shaped, grad_inner)
        back_proj = jnp.einsum('tbo,bio->tbi', grad_inner, left_blocks).reshape(tok_count, D)
        grad_rows = (upstream_rows + back_proj).astype(jnp.bfloat16)
        return ((grad_left, grad_right), (mixed_rows, grad_rows))
    blocked = tokens.reshape(TOKENS // TOK_DEV, TOK_DEV, D)
    blocked_up = upstream.reshape(TOKENS // TOK_DEV, TOK_DEV, D)
    zeros_left = jnp.zeros((BLOCKS, BLK, BLK), jnp.float32)
    zeros_right = jnp.zeros((BLOCKS, BLK, BLK), jnp.float32)
    carried, outputs = lax.scan(block_step, (zeros_left, zeros_right), (blocked, blocked_up))
    scale = 1.0 / math.sqrt(TOKENS)
    mixed = outputs[0].reshape(TOKENS, D)
    grad_tokens = outputs[1].reshape(TOKENS, D)
    return (mixed, grad_tokens, carried[0] * scale, carried[1] * scale)
```

```python
import functools
import math

import jax
import jax.numpy as jnp
from jax import lax
from jax.experimental import pallas as pl
from jax.experimental.pallas import tpu as pltpu
from jax.sharding import PartitionSpec as P

BLOCKS = 32
BLK = 256
NZ, NH, NX = 8, 2, 4
MESH = pl.DeviceIdType.MESH


def place():
    me = lax.axis_index("dp")
    return me // (NH * NX), (me // NX) % NH, me % NX


def dp_of(z, h, x):
    return (z * NH + h) * NX + x


def x_peers(x):
    return x + 1 - 2 * (x % 2), NX - 1 - x, (x + 2) % NX


def greet(z, h, x):
    near, far, _ = x_peers(x)
    peers = [dp_of(z, 1 - h, x), dp_of(z, h, near), dp_of(z, h, far)]
    peers += [dp_of((z + k) % NZ, h, x) for k in range(1, NZ)]
    barrier = pltpu.get_barrier_semaphore()
    for peer in peers:
        pl.semaphore_signal(barrier, inc=1, device_id={"dp": peer}, device_id_type=MESH)
    pl.semaphore_wait(barrier, len(peers))


def push(src, dst, sems, k, peer):
    return pltpu.make_async_remote_copy(
        src_ref=src, dst_ref=dst, send_sem=sems.at[0, k], recv_sem=sems.at[1, k],
        device_id={"dp": peer}, device_id_type=MESH,
    )


def gather_kernel(s_ref, o_ref, buf, sems, lsem):
    z, h, x = place()
    near, far, opp = x_peers(x)
    own = pltpu.make_async_copy(s_ref, buf.at[x, z, h], lsem.at[0])
    own.start()
    greet(z, h, x)
    step_y = push(s_ref, buf.at[x, z, h], sems, 0, dp_of(z, 1 - h, x))
    step_y.start()
    own.wait()
    step_y.wait()
    steps = []
    for k in range(1, NZ):
        c = push(buf.at[x, z], buf.at[x, z], sems, k, dp_of((z + k) % NZ, h, x))
        c.start()
        steps.append(c)
    for c in steps:
        c.wait()
    lo, hi = pl.ds(0, NZ // 2), pl.ds(NZ // 2, NZ // 2)
    to_near, to_far = dp_of(z, h, near), dp_of(z, h, far)
    n_lo = push(buf.at[x, lo], buf.at[x, lo], sems, 8, to_near)
    n_hi = push(buf.at[x, hi], buf.at[x, hi], sems, 9, to_near)
    f_hi = push(buf.at[x, hi], buf.at[x, hi], sems, 10, to_far)
    f_lo = push(buf.at[x, lo], buf.at[x, lo], sems, 11, to_far)
    n_lo.start()
    f_hi.start()
    n_hi.start()
    f_lo.start()
    n_lo.wait_recv()
    r_lo = push(buf.at[near, lo], buf.at[near, lo], sems, 12, to_far)
    r_lo.start()
    f_hi.wait_recv()
    r_hi = push(buf.at[far, hi], buf.at[far, hi], sems, 13, to_near)
    r_hi.start()
    n_hi.wait_recv()
    f_lo.wait_recv()
    r_lo.wait_recv()
    r_hi.wait_recv()
    for c in (n_lo, n_hi, f_hi, f_lo, r_lo, r_hi):
        c.wait_send()
    out = pltpu.make_async_copy(buf, o_ref, lsem.at[1])
    out.start()
    out.wait()


def gather(shard):
    rows = shard.shape[0]
    return pl.pallas_call(
        gather_kernel,
        out_shape=jax.ShapeDtypeStruct((NX, NZ, NH, rows, BLK), shard.dtype),
        in_specs=[pl.BlockSpec(memory_space=pltpu.VMEM)],
        out_specs=pl.BlockSpec(memory_space=pl.ANY),
        scratch_shapes=[
            pltpu.VMEM((NX, NZ, NH, rows, BLK), shard.dtype),
            pltpu.SemaphoreType.DMA((2, 14)),
            pltpu.SemaphoreType.DMA((2,)),
        ],
        compiler_params=pltpu.CompilerParams(collective_id=0, has_side_effects=True),
        name="gather_rows",
    )(shard)


def scatter_kernel(scale, g_ref, o_ref, s1, r1, s2, r2, s3, r3, t, s4, r4, sems):
    z, h, x = place()
    near, far, opp = x_peers(x)
    half = NZ // 2
    for k in range(2):
        zs = pl.ds(k * half, half)
        first = near if k == 0 else far
        s1[k, 0] = g_ref[first, zs].astype(jnp.bfloat16)
        s1[k, 1] = g_ref[opp, zs].astype(jnp.bfloat16)
    greet(z, h, x)
    peer = (dp_of(z, h, near), dp_of(z, h, far))
    ones = []
    for k in range(2):
        c = push(s1.at[k], r1.at[k], sems, k, peer[k])
        c.start()
        ones.append(c)
    twos = []
    for k in range(2):
        ones[k].wait_recv()
        zs = pl.ds(k * half, half)
        second = far if k == 0 else near
        s2[k] = (g_ref[second, zs] + r1[k, 1].astype(jnp.float32)).astype(jnp.bfloat16)
        c = push(s2.at[k], r2.at[k], sems, 2 + k, peer[1 - k])
        c.start()
        twos.append(c)
    for k in range(2):
        twos[k].wait_recv()
        zs = pl.ds(k * half, half)
        t[zs] = g_ref[x, zs] + r1[k, 0].astype(jnp.float32) + r2[k].astype(jnp.float32)
    s3[...] = t[...].astype(jnp.bfloat16)
    threes = []
    for k in range(1, NZ):
        to = (z + k) % NZ
        c = push(s3.at[to], r3.at[k - 1], sems, 3 + k, dp_of(to, h, x))
        c.start()
        threes.append(c)
    total = t[z]
    for k in range(1, NZ):
        threes[k - 1].wait_recv()
        total = total + r3[k - 1].astype(jnp.float32)
    t[0] = total
    s4[...] = t[0, 1 - h]
    last = push(s4, r4, sems, 11, dp_of(z, 1 - h, x))
    last.start()
    last.wait_recv()
    o_ref[...] = (t[0, h] + r4[...]) * scale
    for c in ones + twos + threes + [last]:
        c.wait_send()


def scatter(terms, scale):
    rows = terms.shape[3]
    half = NZ // 2
    tail = (NH, rows, BLK)
    bf, f32 = jnp.bfloat16, jnp.float32
    return pl.pallas_call(
        functools.partial(scatter_kernel, scale),
        out_shape=jax.ShapeDtypeStruct((rows, BLK), f32),
        in_specs=[pl.BlockSpec(memory_space=pltpu.VMEM)],
        out_specs=pl.BlockSpec(memory_space=pltpu.VMEM),
        scratch_shapes=[
            pltpu.VMEM((2, 2, half) + tail, bf),
            pltpu.VMEM((2, 2, half) + tail, bf),
            pltpu.VMEM((2, half) + tail, bf),
            pltpu.VMEM((2, half) + tail, bf),
            pltpu.VMEM((NZ,) + tail, bf),
            pltpu.VMEM((NZ - 1,) + tail, bf),
            pltpu.VMEM((NZ,) + tail, f32),
            pltpu.VMEM((rows, BLK), f32),
            pltpu.VMEM((rows, BLK), f32),
            pltpu.SemaphoreType.DMA((2, 12)),
        ],
        compiler_params=pltpu.CompilerParams(collective_id=1, has_side_effects=True),
        name="scatter_sums",
    )(terms)


def gelu_exact(value):
    return jax.nn.gelu(value, approximate=False)


def add_rows(acts, shard_rows):
    return jnp.einsum("tbi,bio->tbo", acts, shard_rows, preferred_element_type=jnp.float32)


def on_device(tokens, upstream, first_factor, second_factor):
    tok_count = tokens.shape[0]
    local_blocks = first_factor.shape[0]
    own_rows = first_factor.shape[1]
    group_count = lax.axis_size("mp")
    slice_width = BLK // group_count
    inner_span = BLK // BLOCKS
    scale = 1.0 / math.sqrt(tok_count * lax.axis_size("dp"))
    shard = jnp.stack([first_factor, second_factor]).reshape(2 * local_blocks * own_rows, BLK)
    rows = gather(shard).reshape(NX, NZ, NH, 2, local_blocks, own_rows, BLK)
    rows = jnp.transpose(rows, (3, 4, 1, 2, 0, 5, 6)).reshape(2, local_blocks, BLK, BLK)
    first_rows, second_rows = rows[0], rows[1]
    acts = tokens.reshape(tok_count, local_blocks, BLK)
    first_out = add_rows(acts, first_rows).astype(jnp.bfloat16)
    outgoing = jnp.transpose(
        first_out.reshape(tok_count, local_blocks, group_count, slice_width), (2, 0, 1, 3)
    )
    outgoing = outgoing.reshape(group_count, tok_count, local_blocks * slice_width)
    incoming = lax.all_to_all(outgoing, "mp", split_axis=0, concat_axis=0, tiled=True)
    moved_in = incoming.reshape(group_count, tok_count, local_blocks, local_blocks, inner_span)
    moved_in = jnp.transpose(moved_in, (1, 3, 4, 0, 2)).reshape(tok_count, local_blocks, BLK)
    second_out = add_rows(moved_in, second_rows)
    activated, pullback = jax.vjp(gelu_exact, second_out)
    mixed = (tokens.astype(jnp.float32) + activated.reshape(tok_count, local_blocks * BLK)).astype(
        jnp.bfloat16
    )
    upstream_rows = upstream.astype(jnp.float32)
    grad_out = pullback(upstream_rows.reshape(tok_count, local_blocks, BLK))[0].astype(jnp.bfloat16)
    right_term = jnp.einsum("tjc,tjk->jck", moved_in, grad_out, preferred_element_type=jnp.float32)
    grad_moved = jnp.einsum(
        "tjk,jck->tjc", grad_out, second_rows, preferred_element_type=jnp.float32
    )
    grad_moved = grad_moved.astype(jnp.bfloat16)
    returning = grad_moved.reshape(tok_count, local_blocks, inner_span, group_count, local_blocks)
    returning = jnp.transpose(returning, (3, 0, 4, 1, 2)).reshape(
        group_count, tok_count, local_blocks * slice_width
    )
    arrived = lax.all_to_all(returning, "mp", split_axis=0, concat_axis=0, tiled=True)
    grad_inner = jnp.transpose(
        arrived.reshape(group_count, tok_count, local_blocks, slice_width), (1, 2, 0, 3)
    )
    grad_inner = grad_inner.reshape(tok_count, local_blocks, BLK)
    left_term = jnp.einsum("tbi,tbo->bio", acts, grad_inner, preferred_element_type=jnp.float32)
    terms = jnp.stack([left_term, right_term])
    terms = terms.reshape(2, local_blocks, NZ, NH, NX, own_rows, BLK)
    terms = jnp.transpose(terms, (4, 2, 3, 0, 1, 5, 6))
    terms = terms.reshape(NX, NZ, NH, 2 * local_blocks * own_rows, BLK)
    sums = scatter(terms, scale).reshape(2, local_blocks, own_rows, BLK)
    back_proj = jnp.einsum(
        "tbo,bio->tbi", grad_inner, first_rows, preferred_element_type=jnp.float32
    )
    grad_tokens = (upstream_rows + back_proj.reshape(tok_count, local_blocks * BLK)).astype(
        jnp.bfloat16
    )
    return (mixed, grad_tokens, sums[0], sums[1])


def solution(mesh):
    placed = (P("dp", "mp"), P("dp", "mp"), P("mp", "dp", None), P("mp", "dp", None))
    return jax.shard_map(
        on_device,
        mesh=mesh,
        in_specs=placed,
        out_specs=placed,
        check_vma=False,
    )
```

```python
import functools
import math

import jax
import jax.numpy as jnp
from jax import lax
from jax.experimental import pallas as pl
from jax.experimental.pallas import tpu as pltpu
from jax.sharding import PartitionSpec as P

BLK = 256
LOC = 4
ROWS = 4
NZ, NH, NX = 8, 2, 4
NY, NC = 4, 2
NM = NY * NC
FEAT = LOC * BLK
CHUNKS = 4
HALF = NZ // 2
BF, F32 = jnp.bfloat16, jnp.float32
MESH = pl.DeviceIdType.MESH


def dp_of(z, h, x):
    return (z * NH + h) * NX + x


def nn(a, b):
    return lax.dot_general(a, b, (((1,), (0,)), ((), ())), preferred_element_type=F32)


def nt(a, b):
    return lax.dot_general(a, b, (((1,), (1,)), ((), ())), preferred_element_type=F32)


def tn(a, b):
    return lax.dot_general(a, b, (((0,), (0,)), ((), ())), preferred_element_type=F32)


def natural_of_send(s):
    return ((s >> 5) & 3) * 256 + (s >> 7) * 32 + (s & 31)


def arrived_of_sorted(v):
    j, x, oo, h, b = v >> 8, (v >> 6) & 3, (v >> 3) & 7, (v >> 2) & 1, v & 3
    return (h * 4 + x) * 128 + b * 32 + j * 8 + oo


def natural_of_gathered(p):
    return ((p >> 2) & 3) * 256 + ((p >> 4) & 15) * 16 + (p >> 8) * 4 + (p & 3)


def sorted_of_gathered(p):
    return ((p >> 2) & 3) * 256 + (p >> 8) * 64 + ((p >> 4) & 15) * 4 + (p & 3)


def natural_of_sorted(s):
    return ((s >> 2) & 15) * 16 + (s >> 6) * 4 + (s & 3)


def write_perm(ref, source_of):
    rows, cols = ref.shape
    source = source_of(lax.broadcasted_iota(jnp.int32, (1, cols), 1))

    @pl.loop(0, rows // 128)
    def _(k):
        at = pl.ds(pl.multiple_of(k * 128, 128), 128)
        row = lax.broadcasted_iota(jnp.int32, (128, cols), 0) + k * 128
        ref[at, :] = jnp.where(row == source, 1.0, 0.0).astype(BF)


def kernel(
    scale, x_ref, up_ref, shard_ref,
    mixed_ref, gtok_ref, gfac_ref,
    buf, w1, w2, xs, p_send, p_sort, p_nat, p_srt, p_x,
    u_tmp, send_a, recv_a, send_b, recv_b,
    g, s1, r1, s2, r2, t, s3, r3, s4, r4,
    gsem, lsem, sem_a, sem_b, rsem,
):
    me, mp = lax.axis_index("dp"), lax.axis_index("mp")
    z, h, x = me // (NH * NX), (me // NX) % NH, me % NX
    near, far, opp = x + 1 - 2 * (x % 2), NX - 1 - x, (x + 2) % NX
    yl, core = mp // NC, mp % NC
    ys = (yl, yl + 1 - 2 * (yl % 2), NY - 1 - yl, (yl + 2) % NY)
    mates = [ys[0] * NC + 1 - core]
    for k in (1, 2, 3):
        mates += [ys[k] * NC + core, ys[k] * NC + 1 - core]
    to_y, to_near, to_far = dp_of(z, 1 - h, x), dp_of(z, h, near), dp_of(z, h, far)
    to_z = [dp_of((z + k) % NZ, h, x) for k in range(1, NZ)]
    tc = x_ref.shape[0] // CHUNKS

    def push(src, dst, sems, k, peer):
        return pltpu.make_async_remote_copy(
            src_ref=src, dst_ref=dst, send_sem=sems.at[0, k], recv_sem=sems.at[1, k],
            device_id={"dp": peer}, device_id_type=MESH,
        )

    def swap(src, dst, sems, c, k):
        return pltpu.make_async_remote_copy(
            src_ref=src, dst_ref=dst, send_sem=sems.at[0, c, k], recv_sem=sems.at[1, c, k],
            device_id={"mp": mates[k]}, device_id_type=MESH,
        )

    def own(f):
        return pltpu.make_async_copy(shard_ref.at[f], buf.at[f, x, z, h], lsem.at[f])

    def gather_h(f):
        return push(shard_ref.at[f], buf.at[f, x, z, h], gsem.at[f], 0, to_y)

    def gather_z(f):
        part = buf.at[f, x, z]
        return [push(part, part, gsem.at[f], k, to_z[k - 1]) for k in range(1, NZ)]

    def gather_x(f):
        halves = [pl.ds(0, HALF), pl.ds(HALF, HALF)]

        def one(slot, half, k, peer):
            part = buf.at[f, slot, halves[half]]
            return push(part, part, gsem.at[f], k, peer)

        first = [one(x, 0, 8, to_near), one(x, 1, 9, to_far), one(x, 1, 10, to_near), one(x, 0, 11, to_far)]
        return first, lambda: [one(near, 0, 12, to_far), one(far, 1, 13, to_near)]

    def start(copies):
        for c in copies:
            c.start()

    def wait(copies):
        for c in copies:
            c.wait()

    for f in range(2):
        own(f).start()
    barrier = pltpu.get_barrier_semaphore()
    for peer in [to_y, to_near, to_far] + to_z:
        pl.semaphore_signal(barrier, inc=1, device_id={"dp": peer}, device_id_type=MESH)
    for mate in mates:
        pl.semaphore_signal(barrier, inc=1, device_id={"mp": mate}, device_id_type=MESH)
    pl.semaphore_wait(barrier, 3 + len(to_z) + len(mates))
    for f in range(2):
        gather_h(f).start()
    for f in range(2):
        own(f).wait()
    write_perm(p_x, natural_of_sorted)
    for f in range(2):
        gather_h(f).wait()
        start(gather_z(f))
    write_perm(p_nat, natural_of_gathered)
    write_perm(p_send, natural_of_send)
    wait(gather_z(0))
    first, relays = gather_x(0)
    relay = relays()
    start(first)
    write_perm(p_sort, arrived_of_sorted)
    for k in range(2):
        first[k].wait_recv()
        relay[k].start()
    write_perm(p_srt, sorted_of_gathered)
    g[...] = jnp.zeros_like(g)
    for k in range(2):
        first[2 + k].wait_recv()
        relay[k].wait_recv()
    for c in first + relay:
        c.wait_send()
    wait(gather_z(1))
    start(gather_x(1)[0])

    def sort_rows(f, perm, dest):
        rows = buf[f].reshape(FEAT, BLK)
        for b in range(LOC):
            dest[b] = nn(perm[b * BLK : (b + 1) * BLK, :], rows).astype(BF)

    sort_rows(0, p_nat, w1)

    def chunk(c):
        return pl.ds(pl.multiple_of(c * tc, tc), tc)

    def block(b):
        return slice(b * BLK, (b + 1) * BLK)

    def spread(values, send, recv, sems, c):
        for n in range(NM):
            send[c, n] = values(n)
        for k in range(NM - 1):
            swap(send.at[c, mates[k]], recv.at[c, mp], sems, c, k).start()
        recv[c, mp] = send[c, mp]

    def collect(recv, send, sems, c):
        for k in range(NM - 1):
            swap(send.at[c, mates[k]], recv.at[c, mates[k]], sems, c, k).wait_recv()
        return jnp.concatenate([recv[c, n] for n in range(NM)], axis=1)

    def permuted_send(perm_tile, send, recv, sems, c):
        done = {}

        def lanes(n):
            if n % 2 == 0:
                done[0] = perm_tile(n // 2).astype(BF)
            return done[0][:, (n % 2) * 128 : (n % 2 + 1) * 128]

        spread(lanes, send, recv, sems, c)

    @pl.loop(0, CHUNKS)
    def _(c):
        at = chunk(c)
        for b in range(LOC):
            u_tmp[:, block(b)] = nn(x_ref[at, block(b)], w1[b]).astype(BF)
        permuted_send(lambda k: nn(u_tmp[...], p_send[:, block(k)]), send_a, recv_a, sem_a, c)

        @pl.when(c == 1)
        def _():
            first, relays = gather_x(1)
            relay = relays()
            for k in range(2):
                first[k].wait_recv()
                relay[k].start()

        for b in range(LOC):
            xs[at, block(b)] = nn(x_ref[at, block(b)], p_x[...]).astype(BF)

    first, relays = gather_x(1)
    relay = relays()
    for k in range(2):
        first[2 + k].wait_recv()
        relay[k].wait_recv()
    for c in first + relay:
        c.wait_send()
    sort_rows(1, p_srt, w2)

    @pl.loop(0, CHUNKS)
    def _(c):
        at = chunk(c)
        arrived = collect(recv_a, send_a, sem_a, c)
        for j in range(LOC):
            v = nn(arrived, p_sort[:, block(j)]).astype(BF)
            y = nn(v, w2[j])
            cdf = 0.5 * (1.0 + lax.erf(y * math.sqrt(0.5)))
            mixed_ref[at, block(j)] = (x_ref[at, block(j)].astype(F32) + y * cdf).astype(BF)
            slope = cdf + y * (jnp.exp(-0.5 * y * y) * (1.0 / math.sqrt(2.0 * math.pi)))
            cot = (up_ref[at, block(j)].astype(F32) * slope).astype(BF)
            g[1, j] += tn(v, cot).reshape(NX, 2, 32, BLK)
            u_tmp[:, block(j)] = nt(cot, w2[j]).astype(BF)
        permuted_send(lambda k: nt(u_tmp[...], p_sort[block(k), :]), send_b, recv_b, sem_b, c)

    peer = (to_near, to_far)

    def sum_x1(f, k):
        return push(s1.at[f, k], r1.at[f, k], rsem.at[f], k, peer[k])

    def sum_x2(f, k):
        return push(s2.at[f, k], r2.at[f, k], rsem.at[f], 2 + k, peer[1 - k])

    def sum_z(f):
        return [push(s3.at[f, (z + k) % NZ], r3.at[f, k - 1], rsem.at[f], 3 + k, to_z[k - 1]) for k in range(1, NZ)]

    def sum_h(f):
        return push(s4.at[f], r4.at[f], rsem.at[f], 11, to_y)

    def reduce_x1(f):
        for k in range(2):
            s1[f, k, 0] = g[f, :, (near, far)[k], k].astype(BF)
            s1[f, k, 1] = g[f, :, opp, k].astype(BF)
            sum_x1(f, k).start()

    def reduce_x2(f):
        for k in range(2):
            sum_x1(f, k).wait_recv()
            s2[f, k] = (g[f, :, (far, near)[k], k] + r1[f, k, 1].astype(F32)).astype(BF)
            sum_x2(f, k).start()

    def reduce_z(f):
        for k in range(2):
            sum_x2(f, k).wait_recv()
            part = g[f, :, x, k] + r1[f, k, 0].astype(F32) + r2[f, k].astype(F32)
            t[f, :, k * HALF : (k + 1) * HALF] = part.reshape(LOC, HALF, NH * ROWS, BLK)
        for k in range(NZ):
            s3[f, k] = t[f, :, k].reshape(LOC * NH * ROWS, BLK).astype(BF)
        start(sum_z(f))

    def reduce_h(f):
        total = t[f, :, z].reshape(LOC * NH * ROWS, BLK)
        copies = sum_z(f)
        for k in range(NZ - 1):
            copies[k].wait_recv()
            total = total + r3[f, k].astype(F32)
        s4[f] = total
        sum_h(f).start()

    def reduce_end(f):
        sum_h(f).wait_recv()
        total = ((s4[f] + r4[f]) * scale).reshape(LOC, NH * ROWS, BLK)
        gfac_ref[f] = jnp.where(h == 0, total[:, :ROWS], total[:, ROWS:])
        for k in range(2):
            sum_x1(f, k).wait_send()
            sum_x2(f, k).wait_send()
        for c in sum_z(f):
            c.wait_send()
        sum_h(f).wait_send()

    reduce_x1(1)

    @pl.loop(0, CHUNKS)
    def _(c):
        at = chunk(c)
        arrived = collect(recv_b, send_b, sem_b, c)
        for b in range(LOC):
            du = nt(arrived, p_send[block(b), :]).astype(BF)
            g[0, b] += tn(xs[at, block(b)], du).reshape(NX, 2, 32, BLK)
            back = nt(du, w1[b])
            gtok_ref[at, block(b)] = (up_ref[at, block(b)].astype(F32) + back).astype(BF)
        for step, run in enumerate((reduce_x2, reduce_z, reduce_h)):
            pl.when(c == step)(functools.partial(run, 1))

    for run in (reduce_x1, reduce_x2, reduce_z, reduce_h):
        run(0)
    reduce_end(1)
    reduce_end(0)

    @pl.loop(0, CHUNKS)
    def _(c):
        for k in range(NM - 1):
            swap(send_a.at[c, mates[k]], recv_a.at[c, mp], sem_a, c, k).wait_send()
            swap(send_b.at[c, mates[k]], recv_b.at[c, mp], sem_b, c, k).wait_send()


def on_device(tokens, upstream, first_factor, second_factor):
    tok = tokens.shape[0]
    tc = tok // CHUNKS
    scale = 1.0 / math.sqrt(tok * lax.axis_size("dp"))
    shard = jnp.stack([first_factor, second_factor]).reshape(2, LOC * ROWS, BLK)
    vmem = pl.BlockSpec(memory_space=pltpu.VMEM)
    dma = pltpu.SemaphoreType.DMA
    slot = NH * ROWS
    mixed, gtok, gfac = pl.pallas_call(
        functools.partial(kernel, scale),
        out_shape=(
            jax.ShapeDtypeStruct((tok, FEAT), BF),
            jax.ShapeDtypeStruct((tok, FEAT), BF),
            jax.ShapeDtypeStruct((2, LOC, ROWS, BLK), F32),
        ),
        in_specs=[vmem, vmem, vmem],
        out_specs=(vmem, vmem, vmem),
        scratch_shapes=[
            pltpu.VMEM((2, NX, NZ, NH, LOC * ROWS, BLK), BF),
            pltpu.VMEM((LOC, BLK, BLK), BF),
            pltpu.VMEM((LOC, BLK, BLK), BF),
            pltpu.VMEM((tok, FEAT), BF),
            pltpu.VMEM((FEAT, FEAT), BF),
            pltpu.VMEM((FEAT, FEAT), BF),
            pltpu.VMEM((FEAT, FEAT), BF),
            pltpu.VMEM((FEAT, FEAT), BF),
            pltpu.VMEM((BLK, BLK), BF),
            pltpu.VMEM((tc, FEAT), BF),
            pltpu.VMEM((CHUNKS, NM, tc, 128), BF),
            pltpu.VMEM((CHUNKS, NM, tc, 128), BF),
            pltpu.VMEM((CHUNKS, NM, tc, 128), BF),
            pltpu.VMEM((CHUNKS, NM, tc, 128), BF),
            pltpu.VMEM((2, LOC, NX, 2, HALF * slot, BLK), F32),
            pltpu.VMEM((2, 2, 2, LOC, HALF * slot, BLK), BF),
            pltpu.VMEM((2, 2, 2, LOC, HALF * slot, BLK), BF),
            pltpu.VMEM((2, 2, LOC, HALF * slot, BLK), BF),
            pltpu.VMEM((2, 2, LOC, HALF * slot, BLK), BF),
            pltpu.VMEM((2, LOC, NZ, slot, BLK), F32),
            pltpu.VMEM((2, NZ, LOC * slot, BLK), BF),
            pltpu.VMEM((2, NZ - 1, LOC * slot, BLK), BF),
            pltpu.VMEM((2, LOC * slot, BLK), F32),
            pltpu.VMEM((2, LOC * slot, BLK), F32),
            dma((2, 2, 14)),
            dma((2,)),
            dma((2, CHUNKS, NM - 1)),
            dma((2, CHUNKS, NM - 1)),
            dma((2, 2, 12)),
        ],
        compiler_params=pltpu.CompilerParams(
            collective_id=0, has_side_effects=True, vmem_limit_bytes=60 * 1024 * 1024
        ),
        name="monarch_layer",
    )(tokens, upstream, shard)
    return (mixed, gtok, gfac[0], gfac[1])


def solution(mesh):
    placed = (P("dp", "mp"), P("dp", "mp"), P("mp", "dp", None), P("mp", "dp", None))
    return jax.shard_map(
        on_device, mesh=mesh, in_specs=placed, out_specs=placed, check_vma=False
    )
```

```python
import functools
import math

import jax
import jax.numpy as jnp
from jax import lax
from jax.experimental import pallas as pl
from jax.experimental.pallas import tpu as pltpu
from jax.sharding import PartitionSpec as P

BLK = 256
LOC = 4
ROWS = 4
NZ, NH, NX = 8, 2, 4
DP = NZ * NH * NX
NY, NC = 4, 2
NM = NY * NC
FEAT = LOC * BLK
CHUNKS = 4
HALF = NZ // 2
BF, F32 = jnp.bfloat16, jnp.float32
MESH = pl.DeviceIdType.MESH


def dp_of(z, h, x):
    return (z * NH + h) * NX + x


def nn(a, b):
    return lax.dot_general(a, b, (((1,), (0,)), ((), ())), preferred_element_type=F32)


def nt(a, b):
    return lax.dot_general(a, b, (((1,), (1,)), ((), ())), preferred_element_type=F32)


def tn(a, b):
    return lax.dot_general(a, b, (((0,), (0,)), ((), ())), preferred_element_type=F32)


def natural_of_send(s):
    return ((s >> 5) & 3) * 256 + (s >> 7) * 32 + (s & 31)


def arrived_of_sorted(v):
    j, x, oo, h, b = v >> 8, (v >> 6) & 3, (v >> 3) & 7, (v >> 2) & 1, v & 3
    return (h * 4 + x) * 128 + b * 32 + j * 8 + oo


def natural_of_gathered(p):
    return ((p >> 2) & 3) * 256 + ((p >> 4) & 15) * 16 + (p >> 8) * 4 + (p & 3)


def sorted_of_gathered(p):
    return ((p >> 2) & 3) * 256 + (p >> 8) * 64 + ((p >> 4) & 15) * 4 + (p & 3)


def natural_of_sorted(s):
    return ((s >> 2) & 15) * 16 + (s >> 6) * 4 + (s & 3)


def write_perm(ref, source_of):
    rows, cols = ref.shape
    source = source_of(lax.broadcasted_iota(jnp.int32, (1, cols), 1))

    @pl.loop(0, rows // 128)
    def _(k):
        at = pl.ds(pl.multiple_of(k * 128, 128), 128)
        row = lax.broadcasted_iota(jnp.int32, (128, cols), 0) + k * 128
        ref[at, :] = jnp.where(row == source, 1.0, 0.0).astype(BF)


def kernel(
    scale, x_hbm, up_hbm, first_ref, second_ref,
    mixed_ref, gtok_ref, gfirst_ref, gsecond_ref,
    x_ref, up_ref, buf, w1, w2, xs, p_send, p_sort, p_nat, p_srt, p_x,
    u_tmp, send_a, recv_a, send_b, recv_b,
    g, s1, r1, s2, r2, t, s3, r3, s4, r4, s5, r5,
    lsem, gsem, sem_a, sem_b, rsem, fsem,
):
    me, mp = lax.axis_index("dp"), lax.axis_index("mp")
    z, h, x = me // (NH * NX), (me // NX) % NH, me % NX
    near, far, opp = x + 1 - 2 * (x % 2), NX - 1 - x, (x + 2) % NX
    yl, core = mp // NC, mp % NC
    ys = (yl, yl + 1 - 2 * (yl % 2), NY - 1 - yl, (yl + 2) % NY)
    mates = [ys[0] * NC + 1 - core]
    for k in (1, 2, 3):
        mates += [ys[k] * NC + core, ys[k] * NC + 1 - core]
    to_y, to_near, to_far = dp_of(z, 1 - h, x), dp_of(z, h, near), dp_of(z, h, far)
    to_z = [dp_of((z + k) % NZ, h, x) for k in range(1, NZ)]
    tc = x_ref.shape[0] // CHUNKS

    def push(src, dst, sems, k, peer):
        return pltpu.make_async_remote_copy(
            src_ref=src, dst_ref=dst, send_sem=sems.at[0, k], recv_sem=sems.at[1, k],
            device_id={"dp": peer}, device_id_type=MESH,
        )

    def swap(src, dst, sems, c, k):
        return pltpu.make_async_remote_copy(
            src_ref=src, dst_ref=dst, send_sem=sems.at[0, c, k], recv_sem=sems.at[1, c, k],
            device_id={"mp": mates[k]}, device_id_type=MESH,
        )

    def gather_h(f):
        part = buf.at[f, x, z, h]
        return push(part, part, gsem.at[f], 0, to_y)

    def gather_z(f):
        part = buf.at[f, x, z]
        return [push(part, part, gsem.at[f], k, to_z[k - 1]) for k in range(1, NZ)]

    def gather_x(f):
        halves = [pl.ds(0, HALF), pl.ds(HALF, HALF)]

        def one(slot, half, k, peer):
            part = buf.at[f, slot, halves[half]]
            return push(part, part, gsem.at[f], k, peer)

        first = [one(x, 0, 8, to_near), one(x, 1, 9, to_far), one(x, 1, 10, to_near), one(x, 0, 11, to_far)]
        return first, lambda: [one(near, 0, 12, to_far), one(far, 1, 13, to_near)]

    def start(copies):
        for c in copies:
            c.start()

    def wait(copies):
        for c in copies:
            c.wait()

    load_x = pltpu.make_async_copy(x_hbm, x_ref, lsem.at[0])
    load_up = pltpu.make_async_copy(up_hbm, up_ref, lsem.at[1])
    load_x.start()
    load_up.start()
    for f, ref in enumerate((first_ref, second_ref)):
        rows = [ref[b].astype(F32) for b in range(LOC)]
        buf[f, x, z, h] = jnp.concatenate(rows, axis=0).astype(BF)
    barrier = pltpu.get_barrier_semaphore()
    for peer in [to_y, to_near, to_far] + to_z:
        pl.semaphore_signal(barrier, inc=1, device_id={"dp": peer}, device_id_type=MESH)
    for mate in mates:
        pl.semaphore_signal(barrier, inc=1, device_id={"mp": mate}, device_id_type=MESH)
    pl.semaphore_wait(barrier, 3 + len(to_z) + len(mates))
    for f in range(2):
        gather_h(f).start()
    write_perm(p_x, natural_of_sorted)
    for f in range(2):
        gather_h(f).wait()
        start(gather_z(f))
    write_perm(p_nat, natural_of_gathered)
    write_perm(p_send, natural_of_send)
    wait(gather_z(0))
    first, relays = gather_x(0)
    relay = relays()
    start(first)
    write_perm(p_sort, arrived_of_sorted)
    for k in range(2):
        first[k].wait_recv()
        relay[k].start()
    write_perm(p_srt, sorted_of_gathered)
    g[...] = jnp.zeros_like(g)
    for k in range(2):
        first[2 + k].wait_recv()
        relay[k].wait_recv()
    for c in first + relay:
        c.wait_send()
    wait(gather_z(1))
    start(gather_x(1)[0])

    def sort_rows(f, perm, dest):
        rows = buf[f].reshape(FEAT, BLK)
        for b in range(LOC):
            dest[b] = nn(perm[b * BLK : (b + 1) * BLK, :], rows).astype(BF)

    sort_rows(0, p_nat, w1)
    load_x.wait()

    def chunk(c):
        return pl.ds(pl.multiple_of(c * tc, tc), tc)

    def block(b):
        return slice(b * BLK, (b + 1) * BLK)

    def spread(values, send, recv, sems, c):
        for n in range(NM):
            send[c, n] = values(n)
        for k in range(NM - 1):
            swap(send.at[c, mates[k]], recv.at[c, mp], sems, c, k).start()
        recv[c, mp] = send[c, mp]

    def collect(recv, send, sems, c):
        for k in range(NM - 1):
            swap(send.at[c, mates[k]], recv.at[c, mates[k]], sems, c, k).wait_recv()
        return jnp.concatenate([recv[c, n] for n in range(NM)], axis=1)

    def permuted_send(perm_tile, send, recv, sems, c):
        done = {}

        def lanes(n):
            if n % 2 == 0:
                done[0] = perm_tile(n // 2).astype(BF)
            return done[0][:, (n % 2) * 128 : (n % 2 + 1) * 128]

        spread(lanes, send, recv, sems, c)

    @pl.loop(0, CHUNKS)
    def _(c):
        at = chunk(c)
        for b in range(LOC):
            u_tmp[:, block(b)] = nn(x_ref[at, block(b)], w1[b]).astype(BF)
        permuted_send(lambda k: nn(u_tmp[...], p_send[:, block(k)]), send_a, recv_a, sem_a, c)

        @pl.when(c == 1)
        def _():
            first, relays = gather_x(1)
            relay = relays()
            for k in range(2):
                first[k].wait_recv()
                relay[k].start()

        for b in range(LOC):
            xs[at, block(b)] = nn(x_ref[at, block(b)], p_x[...]).astype(BF)

    first, relays = gather_x(1)
    relay = relays()
    for k in range(2):
        first[2 + k].wait_recv()
        relay[k].wait_recv()
    for c in first + relay:
        c.wait_send()
    sort_rows(1, p_srt, w2)
    load_up.wait()

    @pl.loop(0, CHUNKS)
    def _(c):
        at = chunk(c)
        arrived = collect(recv_a, send_a, sem_a, c)
        for j in range(LOC):
            v = nn(arrived, p_sort[:, block(j)]).astype(BF)
            y = nn(v, w2[j])
            cdf = 0.5 * (1.0 + lax.erf(y * math.sqrt(0.5)))
            mixed_ref[at, block(j)] = (x_ref[at, block(j)].astype(F32) + y * cdf).astype(BF)
            slope = cdf + y * (jnp.exp(-0.5 * y * y) * (1.0 / math.sqrt(2.0 * math.pi)))
            cot = (up_ref[at, block(j)].astype(F32) * slope).astype(BF)
            g[1, j] += tn(v, cot).reshape(NX, 2, 32, BLK)
            u_tmp[:, block(j)] = nt(cot, w2[j]).astype(BF)
        permuted_send(lambda k: nt(u_tmp[...], p_sort[block(k), :]), send_b, recv_b, sem_b, c)

    peer = (to_near, to_far)

    def sum_x1(k):
        return push(s1.at[k], r1.at[k], rsem, k, peer[k])

    def sum_x2(k):
        return push(s2.at[k], r2.at[k], rsem, 2 + k, peer[1 - k])

    def sum_z():
        return [push(s3.at[(z + k) % NZ], r3.at[k - 1], rsem, 3 + k, to_z[k - 1]) for k in range(1, NZ)]

    def sum_h():
        return push(s4, r4, rsem, 11, to_y)

    def reduce_x1():
        for k in range(2):
            s1[k, 0] = g[1, :, (near, far)[k], k].astype(BF)
            s1[k, 1] = g[1, :, opp, k].astype(BF)
            sum_x1(k).start()

    def reduce_x2():
        for k in range(2):
            sum_x1(k).wait_recv()
            s2[k] = (g[1, :, (far, near)[k], k] + r1[k, 1].astype(F32)).astype(BF)
            sum_x2(k).start()

    def reduce_z():
        for k in range(2):
            sum_x2(k).wait_recv()
            part = g[1, :, x, k] + r1[k, 0].astype(F32) + r2[k].astype(F32)
            t[:, k * HALF : (k + 1) * HALF] = part.reshape(LOC, HALF, NH * ROWS, BLK)
        for k in range(NZ):
            s3[k] = t[:, k].reshape(LOC * NH * ROWS, BLK).astype(BF)
        start(sum_z())

    def reduce_h():
        total = t[:, z].reshape(LOC * NH * ROWS, BLK)
        copies = sum_z()
        for k in range(NZ - 1):
            copies[k].wait_recv()
            total = total + r3[k].astype(F32)
        total = total.reshape(LOC, NH * ROWS, BLK)
        s4[...] = jnp.where(h == 0, total[:, ROWS:], total[:, :ROWS])
        gsecond_ref[...] = jnp.where(h == 0, total[:, :ROWS], total[:, ROWS:])
        sum_h().start()

    def reduce_end():
        sum_h().wait_recv()
        gsecond_ref[...] = (gsecond_ref[...] + r4[...]) * scale
        for k in range(2):
            sum_x1(k).wait_send()
            sum_x2(k).wait_send()
        for c in sum_z():
            c.wait_send()
        sum_h().wait_send()

    def final(i):
        to = (me + i) % DP
        return push(s5.at[to], r5.at[i - 1], fsem, i - 1, to)

    def pack_final():
        low = lax.broadcasted_iota(jnp.int32, (NZ, NH * ROWS, BLK), 1) < ROWS
        for xx in range(NX):
            tile = [g[0, b, xx].reshape(NZ, NH * ROWS, BLK) for b in range(LOC)]
            turned = [pltpu.roll(v, ROWS, 1) for v in tile]
            for hh in range(NH):
                pair = []
                for b in (0, 2):
                    if hh == 0:
                        pair.append(jnp.where(low, tile[b], turned[b + 1]))
                    else:
                        pair.append(jnp.where(low, turned[b], tile[b + 1]))
                rows = jnp.concatenate(pair, axis=1).astype(BF)
                for zz in range(NZ):
                    s5[dp_of(zz, hh, xx)] = rows[zz]

    reduce_x1()

    def first_grad(c):
        at = chunk(c)
        arrived = collect(recv_b, send_b, sem_b, c)
        for b in range(LOC):
            du = nt(arrived, p_send[block(b), :]).astype(BF)
            u_tmp[:, block(b)] = du
            g[0, b] += tn(xs[at, block(b)], du).reshape(NX, 2, 32, BLK)

    def token_grad(c):
        at = chunk(c)
        for b in range(LOC):
            back = nt(u_tmp[:, block(b)], w1[b])
            gtok_ref[at, block(b)] = (up_ref[at, block(b)].astype(F32) + back).astype(BF)

    @pl.loop(0, CHUNKS - 1)
    def _(c):
        first_grad(c)
        token_grad(c)
        for step, run in enumerate((reduce_x2, reduce_z, reduce_h)):
            pl.when(c == step)(run)

    first_grad(CHUNKS - 1)
    pack_final()

    @pl.loop(1, DP)
    def _(i):
        final(i).start()

    token_grad(CHUNKS - 1)
    reduce_end()

    @pl.loop(0, CHUNKS)
    def _(c):
        for k in range(NM - 1):
            swap(send_a.at[c, mates[k]], recv_a.at[c, mp], sem_a, c, k).wait_send()
            swap(send_b.at[c, mates[k]], recv_b.at[c, mp], sem_b, c, k).wait_send()

    def add_final(i, total):
        final(i).wait_recv()
        return total + r5[i - 1].astype(F32)

    total = lax.fori_loop(1, DP, add_final, s5[me].astype(F32)) * scale
    for b in range(LOC):
        gfirst_ref[b] = total[b * ROWS : (b + 1) * ROWS]

    @pl.loop(1, DP)
    def _(i):
        final(i).wait_send()


def on_device(tokens, upstream, first_factor, second_factor):
    tok = tokens.shape[0]
    tc = tok // CHUNKS
    scale = 1.0 / math.sqrt(tok * lax.axis_size("dp"))
    vmem = pl.BlockSpec(memory_space=pltpu.VMEM)
    hbm = pl.BlockSpec(memory_space=pltpu.HBM)
    dma = pltpu.SemaphoreType.DMA
    slot = NH * ROWS
    return pl.pallas_call(
        functools.partial(kernel, scale),
        out_shape=(
            jax.ShapeDtypeStruct((tok, FEAT), BF),
            jax.ShapeDtypeStruct((tok, FEAT), BF),
            jax.ShapeDtypeStruct((LOC, ROWS, BLK), F32),
            jax.ShapeDtypeStruct((LOC, ROWS, BLK), F32),
        ),
        in_specs=[hbm, hbm, vmem, vmem],
        out_specs=(vmem,) * 4,
        scratch_shapes=[
            pltpu.VMEM((tok, FEAT), BF),
            pltpu.VMEM((tok, FEAT), BF),
            pltpu.VMEM((2, NX, NZ, NH, LOC * ROWS, BLK), BF),
            pltpu.VMEM((LOC, BLK, BLK), BF),
            pltpu.VMEM((LOC, BLK, BLK), BF),
            pltpu.VMEM((tok, FEAT), BF),
            pltpu.VMEM((FEAT, FEAT), BF),
            pltpu.VMEM((FEAT, FEAT), BF),
            pltpu.VMEM((FEAT, FEAT), BF),
            pltpu.VMEM((FEAT, FEAT), BF),
            pltpu.VMEM((BLK, BLK), BF),
            pltpu.VMEM((tc, FEAT), BF),
            pltpu.VMEM((CHUNKS, NM, tc, 128), BF),
            pltpu.VMEM((CHUNKS, NM, tc, 128), BF),
            pltpu.VMEM((CHUNKS, NM, tc, 128), BF),
            pltpu.VMEM((CHUNKS, NM, tc, 128), BF),
            pltpu.VMEM((2, LOC, NX, 2, HALF * slot, BLK), F32),
            pltpu.VMEM((2, 2, LOC, HALF * slot, BLK), BF),
            pltpu.VMEM((2, 2, LOC, HALF * slot, BLK), BF),
            pltpu.VMEM((2, LOC, HALF * slot, BLK), BF),
            pltpu.VMEM((2, LOC, HALF * slot, BLK), BF),
            pltpu.VMEM((LOC, NZ, slot, BLK), F32),
            pltpu.VMEM((NZ, LOC * slot, BLK), BF),
            pltpu.VMEM((NZ - 1, LOC * slot, BLK), BF),
            pltpu.VMEM((LOC, ROWS, BLK), F32),
            pltpu.VMEM((LOC, ROWS, BLK), F32),
            pltpu.VMEM((DP, LOC * ROWS, BLK), BF),
            pltpu.VMEM((DP - 1, LOC * ROWS, BLK), BF),
            dma((2,)),
            dma((2, 2, 14)),
            dma((2, CHUNKS, NM - 1)),
            dma((2, CHUNKS, NM - 1)),
            dma((2, 12)),
            dma((2, DP - 1)),
        ],
        compiler_params=pltpu.CompilerParams(
            collective_id=0, has_side_effects=True, vmem_limit_bytes=40 * 1024 * 1024
        ),
        name="monarch_layer",
    )(tokens, upstream, first_factor, second_factor)


def solution(mesh):
    placed = (P("dp", "mp"), P("dp", "mp"), P("mp", "dp", None), P("mp", "dp", None))
    return jax.shard_map(
        on_device, mesh=mesh, in_specs=placed, out_specs=placed, check_vma=False
    )
```

```python
import functools
import math

import jax
import jax.numpy as jnp
from jax import lax
from jax.experimental import pallas as pl
from jax.experimental.pallas import tpu as pltpu
from jax.sharding import PartitionSpec as P

BLK = 256
LOC = 4
ROWS = 4
NZ, NH, NX = 8, 2, 4
DP = NZ * NH * NX
NY, NC = 4, 2
NM = NY * NC
FEAT = LOC * BLK
CHUNKS = 4
HALF = NZ // 2
BF, F32 = jnp.bfloat16, jnp.float32
MESH = pl.DeviceIdType.MESH


def dp_of(z, h, x):
    return (z * NH + h) * NX + x


def nn(a, b):
    return lax.dot_general(a, b, (((1,), (0,)), ((), ())), preferred_element_type=F32)


def nt(a, b):
    return lax.dot_general(a, b, (((1,), (1,)), ((), ())), preferred_element_type=F32)


def tn(a, b):
    return lax.dot_general(a, b, (((0,), (0,)), ((), ())), preferred_element_type=F32)


def natural_of_send(s):
    return ((s >> 5) & 3) * 128 + (s >> 7) * 32 + (s & 31)


def arrived_of_sorted(v):
    j, x, oo, h, b = v >> 8, (v >> 6) & 3, (v >> 3) & 7, (v >> 2) & 1, v & 3
    return (h * 4 + x) * 128 + b * 32 + j * 8 + oo


def natural_of_gathered(p):
    return ((p >> 2) & 3) * 256 + ((p >> 4) & 15) * 16 + (p >> 8) * 4 + (p & 3)


def sorted_of_gathered(p):
    return ((p >> 2) & 3) * 256 + (p >> 8) * 64 + ((p >> 4) & 15) * 4 + (p & 3)


def natural_of_sorted(s):
    return ((s >> 2) & 15) * 16 + (s >> 6) * 4 + (s & 3)


def write_perm(ref, source_of):
    rows, cols = ref.shape
    source = source_of(lax.broadcasted_iota(jnp.int32, (1, cols), 1))

    @pl.loop(0, rows // 128)
    def _(k):
        at = pl.ds(pl.multiple_of(k * 128, 128), 128)
        row = lax.broadcasted_iota(jnp.int32, (128, cols), 0) + k * 128
        ref[at, :] = jnp.where(row == source, 1.0, 0.0).astype(BF)


def kernel(
    scale, x_hbm, up_hbm, first_hbm, second_hbm,
    mixed_ref, gtok_ref, gfirst_ref, gsecond_ref,
    x_ref, up_ref, shard, buf_a, buf_b, w1, w2, xs, p_send, p_sort, p_nat, p_srt, p_x,
    u_tmp, send_a, recv_a, send_b, recv_b,
    g, s1, r1, s2, r2, t, s3, r3, s4, r4, s5, r5,
    lsem, gsem, sem_a, sem_b, rsem, fsem,
):
    me, mp = lax.axis_index("dp"), lax.axis_index("mp")
    z, h, x = me // (NH * NX), (me // NX) % NH, me % NX
    near, far, opp = x + 1 - 2 * (x % 2), NX - 1 - x, (x + 2) % NX
    yl, core = mp // NC, mp % NC
    ys = (yl, yl + 1 - 2 * (yl % 2), NY - 1 - yl, (yl + 2) % NY)
    mates = [ys[0] * NC + 1 - core]
    for k in (1, 2, 3):
        mates += [ys[k] * NC + core, ys[k] * NC + 1 - core]
    to_y, to_near, to_far = dp_of(z, 1 - h, x), dp_of(z, h, near), dp_of(z, h, far)
    to_z = [dp_of((z + k) % NZ, h, x) for k in range(1, NZ)]
    tc = x_ref.shape[0] // CHUNKS

    def push(src, dst, sems, k, peer):
        return pltpu.make_async_remote_copy(
            src_ref=src, dst_ref=dst, send_sem=sems.at[0, k], recv_sem=sems.at[1, k],
            device_id={"dp": peer}, device_id_type=MESH,
        )

    def swap(src, dst, sems, c, k):
        return pltpu.make_async_remote_copy(
            src_ref=src, dst_ref=dst, send_sem=sems.at[0, c, k], recv_sem=sems.at[1, c, k],
            device_id={"mp": mates[k]}, device_id_type=MESH,
        )

    bufs = (buf_a.at[0], buf_a.at[1], buf_b)
    sides = (1 - yl // 2, yl // 2)

    def gather_h(f):
        part = bufs[f].at[x, z, h]
        return push(part, part, gsem.at[f], 0, to_y)

    def gather_z(f):
        part = bufs[f].at[x, z]
        return [push(part, part, gsem.at[f], k, to_z[k - 1]) for k in range(1, NZ)]

    def gather_x(f):
        halves = [pl.ds(0, HALF), pl.ds(HALF, HALF)]

        def one(slot, half, k, peer):
            part = bufs[f].at[slot, halves[half]]
            return push(part, part, gsem.at[f], k, peer)

        def first():
            return [one(x, 0, 8, to_near), one(x, 1, 9, to_far)]

        def second():
            return [one(x, 1, 10, to_near), one(x, 0, 11, to_far)]

        def relay():
            return [one(near, 0, 12, to_far), one(far, 1, 13, to_near)]

        return first, second, relay

    def open_x(f):
        first, second, _ = gather_x(f)
        start(first() + second())

    def relay_x(f):
        first, _, relay = gather_x(f)
        for c, onward in zip(first(), relay()):
            c.wait_recv()
            onward.start()

    def close_x(f):
        first, second, relay = gather_x(f)
        rest = second() + relay()
        for c in rest:
            c.wait_recv()
        for c in first() + rest:
            c.wait_send()

    def start(copies):
        for c in copies:
            c.start()

    def wait(copies):
        for c in copies:
            c.wait()

    load_x = pltpu.make_async_copy(x_hbm, x_ref, lsem.at[0])
    load_up = pltpu.make_async_copy(up_hbm, up_ref, lsem.at[1])
    load_rows = [
        pltpu.make_async_copy(ref, shard.at[f], lsem.at[2 + f])
        for f, ref in enumerate((first_hbm, second_hbm))
    ]
    start(load_rows)
    load_x.start()
    load_up.start()
    wait(load_rows)
    for f in range(2):
        rows = [shard[f, b].astype(F32) for b in range(LOC)]
        rows = jnp.concatenate(rows, axis=0)
        if f == 1:
            buf_b[x, z, h] = rows.astype(BF)
        else:
            low, high = rows[:, :128], rows[:, 128:]
            buf_a[0, x, z, h] = jnp.where(yl < NY // 2, high, low).astype(BF)
            buf_a[1, x, z, h] = jnp.where(yl < NY // 2, low, high).astype(BF)
    barrier = pltpu.get_barrier_semaphore()
    for peer in [to_y, to_near, to_far] + to_z:
        pl.semaphore_signal(barrier, inc=1, device_id={"dp": peer}, device_id_type=MESH)
    for mate in mates:
        pl.semaphore_signal(barrier, inc=1, device_id={"mp": mate}, device_id_type=MESH)
    pl.semaphore_wait(barrier, 3 + len(to_z) + len(mates))
    for f in range(3):
        gather_h(f).start()
    write_perm(p_x, natural_of_sorted)
    for f in range(3):
        gather_h(f).wait()
        start(gather_z(f))
    write_perm(p_nat, natural_of_gathered)
    write_perm(p_send, natural_of_send)
    wait(gather_z(0))
    open_x(0)
    wait(gather_z(1))
    write_perm(p_sort, arrived_of_sorted)
    relay_x(0)
    open_x(1)
    write_perm(p_srt, sorted_of_gathered)
    g[...] = jnp.zeros_like(g)
    load_x.wait()
    close_x(0)

    def side_lanes(p):
        return pl.ds(pl.multiple_of(sides[p] * 128, 128), 128)

    def sort_first(p):
        rows = buf_a[p].reshape(FEAT, 128)
        for b in range(LOC):
            w1[b, :, side_lanes(p)] = nn(p_nat[b * BLK : (b + 1) * BLK, :], rows).astype(BF)

    def chunk(c):
        return pl.ds(pl.multiple_of(c * tc, tc), tc)

    def block(b):
        return slice(b * BLK, (b + 1) * BLK)

    def launch(send, recv, sems, c, ks):
        for k in ks:
            swap(send.at[c, mates[k]], recv.at[c, mp], sems, c, k).start()

    def launch_all(send, recv, sems, c):
        launch(send, recv, sems, c, range(NM - 1))
        recv[c, mp] = send[c, mp]

    def collect(recv, send, sems, c):
        for k in range(NM - 1):
            swap(send.at[c, mates[k]], recv.at[c, mates[k]], sems, c, k).wait_recv()
        return jnp.concatenate([recv[c, n] for n in range(NM)], axis=1)

    def send_side(half, side, c):
        lanes = nn(half, p_send[...]).astype(BF)
        for n in range(NM // 2):
            send_a[c, side * (NM // 2) + n] = lanes[:, n * 128 : (n + 1) * 128]

    for p in range(2):
        if p == 1:
            relay_x(1)
            wait(gather_z(2))
            open_x(2)
            close_x(1)
        sort_first(p)
        at = chunk(0)
        half = [nn(x_ref[at, block(b)], w1[b, :, side_lanes(p)]).astype(BF) for b in range(LOC)]
        send_side(jnp.concatenate(half, axis=1), sides[p], 0)
        launch(send_a, recv_a, sem_a, 0, (range(3, NM - 1), range(3))[p])
    recv_a[0, mp] = send_a[0, mp]

    def sort_tokens(at):
        for b in range(LOC):
            xs[at, block(b)] = nn(x_ref[at, block(b)], p_x[...]).astype(BF)

    @pl.loop(1, CHUNKS)
    def _(c):
        at = chunk(c)
        for b in range(LOC):
            u_tmp[:, block(b)] = nn(x_ref[at, block(b)], w1[b]).astype(BF)
        for side in range(2):
            half = [u_tmp[:, b * BLK + side * 128 : b * BLK + side * 128 + 128] for b in range(LOC)]
            send_side(jnp.concatenate(half, axis=1), side, c)
        launch_all(send_a, recv_a, sem_a, c)

        @pl.when(c == 1)
        def _():
            relay_x(2)

        sort_tokens(at)

    sort_tokens(chunk(0))
    close_x(2)
    rows = buf_b[...].reshape(FEAT, BLK)
    for b in range(LOC):
        w2[b] = nn(p_srt[block(b), :], rows).astype(BF)
    load_up.wait()

    @pl.loop(0, CHUNKS)
    def _(c):
        at = chunk(c)
        arrived = collect(recv_a, send_a, sem_a, c)
        for j in range(LOC):
            v = nn(arrived, p_sort[:, block(j)]).astype(BF)
            y = nn(v, w2[j])
            cdf = 0.5 * (1.0 + lax.erf(y * math.sqrt(0.5)))
            mixed_ref[at, block(j)] = (x_ref[at, block(j)].astype(F32) + y * cdf).astype(BF)
            slope = cdf + y * (jnp.exp(-0.5 * y * y) * (1.0 / math.sqrt(2.0 * math.pi)))
            cot = (up_ref[at, block(j)].astype(F32) * slope).astype(BF)
            g[1, j] += tn(v, cot).reshape(NX, 2, 32, BLK)
            u_tmp[:, block(j)] = nt(cot, w2[j]).astype(BF)
        for k in range(LOC):
            lanes = nt(u_tmp[...], p_sort[block(k), :]).astype(BF)
            send_b[c, 2 * k] = lanes[:, :128]
            send_b[c, 2 * k + 1] = lanes[:, 128:]
        launch_all(send_b, recv_b, sem_b, c)

    peer = (to_near, to_far)

    def sum_x1(k):
        return push(s1.at[k], r1.at[k], rsem, k, peer[k])

    def sum_x2(k):
        return push(s2.at[k], r2.at[k], rsem, 2 + k, peer[1 - k])

    def sum_z():
        return [push(s3.at[(z + k) % NZ], r3.at[k - 1], rsem, 3 + k, to_z[k - 1]) for k in range(1, NZ)]

    def sum_h():
        return push(s4, r4, rsem, 11, to_y)

    def reduce_x1():
        for k in range(2):
            s1[k, 0] = g[1, :, (near, far)[k], k].astype(BF)
            s1[k, 1] = g[1, :, opp, k].astype(BF)
            sum_x1(k).start()

    def reduce_x2():
        for k in range(2):
            sum_x1(k).wait_recv()
            s2[k] = (g[1, :, (far, near)[k], k] + r1[k, 1].astype(F32)).astype(BF)
            sum_x2(k).start()

    def reduce_z():
        for k in range(2):
            sum_x2(k).wait_recv()
            part = g[1, :, x, k] + r1[k, 0].astype(F32) + r2[k].astype(F32)
            t[:, k * HALF : (k + 1) * HALF] = part.reshape(LOC, HALF, NH * ROWS, BLK)
        for k in range(NZ):
            s3[k] = t[:, k].reshape(LOC * NH * ROWS, BLK).astype(BF)
        start(sum_z())

    def reduce_h():
        total = t[:, z].reshape(LOC * NH * ROWS, BLK)
        copies = sum_z()
        for k in range(NZ - 1):
            copies[k].wait_recv()
            total = total + r3[k].astype(F32)
        total = total.reshape(LOC, NH * ROWS, BLK)
        s4[...] = jnp.where(h == 0, total[:, ROWS:], total[:, :ROWS])
        gsecond_ref[...] = jnp.where(h == 0, total[:, :ROWS], total[:, ROWS:])
        sum_h().start()

    def reduce_end():
        sum_h().wait_recv()
        gsecond_ref[...] = (gsecond_ref[...] + r4[...]) * scale
        for k in range(2):
            sum_x1(k).wait_send()
            sum_x2(k).wait_send()
        for c in sum_z():
            c.wait_send()
        sum_h().wait_send()

    def final(i):
        to = (me + i) % DP
        return push(s5.at[to], r5.at[i - 1], fsem, i - 1, to)

    def pack_final():
        low = lax.broadcasted_iota(jnp.int32, (NZ, NH * ROWS, BLK), 1) < ROWS
        for xx in range(NX):
            tile = [g[0, b, xx].reshape(NZ, NH * ROWS, BLK) for b in range(LOC)]
            turned = [pltpu.roll(v, ROWS, 1) for v in tile]
            for hh in range(NH):
                pair = []
                for b in (0, 2):
                    if hh == 0:
                        pair.append(jnp.where(low, tile[b], turned[b + 1]))
                    else:
                        pair.append(jnp.where(low, turned[b], tile[b + 1]))
                rows = jnp.concatenate(pair, axis=1).astype(BF)
                for zz in range(NZ):
                    s5[dp_of(zz, hh, xx)] = rows[zz]

    reduce_x1()

    def first_grad(c):
        at = chunk(c)
        arrived = collect(recv_b, send_b, sem_b, c)
        side = [nt(arrived[:, k * 512 : (k + 1) * 512], p_send[...]).astype(BF) for k in range(2)]
        for b in range(LOC):
            du = jnp.concatenate([v[:, b * 128 : (b + 1) * 128] for v in side], axis=1)
            u_tmp[:, block(b)] = du
            g[0, b] += tn(xs[at, block(b)], du).reshape(NX, 2, 32, BLK)

    def token_grad(c):
        at = chunk(c)
        for b in range(LOC):
            back = nt(u_tmp[:, block(b)], w1[b])
            gtok_ref[at, block(b)] = (up_ref[at, block(b)].astype(F32) + back).astype(BF)

    @pl.loop(0, CHUNKS - 1)
    def _(c):
        first_grad(c)
        token_grad(c)
        for step, run in enumerate((reduce_x2, reduce_z, reduce_h)):
            pl.when(c == step)(run)

    first_grad(CHUNKS - 1)
    pack_final()

    @pl.loop(1, DP)
    def _(i):
        final(i).start()

    token_grad(CHUNKS - 1)
    reduce_end()

    @pl.loop(0, CHUNKS)
    def _(c):
        for k in range(NM - 1):
            swap(send_a.at[c, mates[k]], recv_a.at[c, mp], sem_a, c, k).wait_send()
            swap(send_b.at[c, mates[k]], recv_b.at[c, mp], sem_b, c, k).wait_send()

    def add_final(i, total):
        final(i).wait_recv()
        return total + r5[i - 1].astype(F32)

    total = lax.fori_loop(1, DP, add_final, s5[me].astype(F32)) * scale
    for b in range(LOC):
        gfirst_ref[b] = total[b * ROWS : (b + 1) * ROWS]

    @pl.loop(1, DP)
    def _(i):
        final(i).wait_send()


def store_kernel(*refs):
    count = len(refs) // 2
    sems = refs[-1]
    copies = [
        pltpu.make_async_copy(refs[i], refs[count + i], sems.at[i]) for i in range(count)
    ]
    for c in copies:
        c.start()
    for c in copies:
        c.wait()


def store(results):
    count = len(results)
    return pl.pallas_call(
        store_kernel,
        out_shape=tuple(jax.ShapeDtypeStruct(r.shape, r.dtype) for r in results),
        in_specs=[pl.BlockSpec(memory_space=pltpu.VMEM)] * count,
        out_specs=(pl.BlockSpec(memory_space=pltpu.HBM),) * count,
        scratch_shapes=[pltpu.SemaphoreType.DMA((count,))],
        name="store_results",
    )(*(pltpu.with_memory_space_constraint(r, pltpu.VMEM) for r in results))


def on_device(*args):
    tok = args[0].shape[0]
    tc = tok // CHUNKS
    scale = 1.0 / math.sqrt(tok * lax.axis_size("dp"))
    vmem = pl.BlockSpec(memory_space=pltpu.VMEM)
    hbm = pl.BlockSpec(memory_space=pltpu.HBM)
    dma = pltpu.SemaphoreType.DMA
    slot = NH * ROWS
    results = pl.pallas_call(
        functools.partial(kernel, scale),
        out_shape=(
            jax.ShapeDtypeStruct((tok, FEAT), BF),
            jax.ShapeDtypeStruct((tok, FEAT), BF),
            jax.ShapeDtypeStruct((LOC, ROWS, BLK), F32),
            jax.ShapeDtypeStruct((LOC, ROWS, BLK), F32),
        ),
        in_specs=[hbm] * 4,
        out_specs=(vmem,) * 4,
        scratch_shapes=[
            pltpu.VMEM((tok, FEAT), BF),
            pltpu.VMEM((tok, FEAT), BF),
            pltpu.VMEM((2, LOC, ROWS, BLK), BF),
            pltpu.VMEM((2, NX, NZ, NH, LOC * ROWS, 128), BF),
            pltpu.VMEM((NX, NZ, NH, LOC * ROWS, BLK), BF),
            pltpu.VMEM((LOC, BLK, BLK), BF),
            pltpu.VMEM((LOC, BLK, BLK), BF),
            pltpu.VMEM((tok, FEAT), BF),
            pltpu.VMEM((FEAT // 2, FEAT // 2), BF),
            pltpu.VMEM((FEAT, FEAT), BF),
            pltpu.VMEM((FEAT, FEAT), BF),
            pltpu.VMEM((FEAT, FEAT), BF),
            pltpu.VMEM((BLK, BLK), BF),
            pltpu.VMEM((tc, FEAT), BF),
            pltpu.VMEM((CHUNKS, NM, tc, 128), BF),
            pltpu.VMEM((CHUNKS, NM, tc, 128), BF),
            pltpu.VMEM((CHUNKS, NM, tc, 128), BF),
            pltpu.VMEM((CHUNKS, NM, tc, 128), BF),
            pltpu.VMEM((2, LOC, NX, 2, HALF * slot, BLK), F32),
            pltpu.VMEM((2, 2, LOC, HALF * slot, BLK), BF),
            pltpu.VMEM((2, 2, LOC, HALF * slot, BLK), BF),
            pltpu.VMEM((2, LOC, HALF * slot, BLK), BF),
            pltpu.VMEM((2, LOC, HALF * slot, BLK), BF),
            pltpu.VMEM((LOC, NZ, slot, BLK), F32),
            pltpu.VMEM((NZ, LOC * slot, BLK), BF),
            pltpu.VMEM((NZ - 1, LOC * slot, BLK), BF),
            pltpu.VMEM((LOC, ROWS, BLK), F32),
            pltpu.VMEM((LOC, ROWS, BLK), F32),
            pltpu.VMEM((DP, LOC * ROWS, BLK), BF),
            pltpu.VMEM((DP - 1, LOC * ROWS, BLK), BF),
            dma((4,)),
            dma((3, 2, 14)),
            dma((2, CHUNKS, NM - 1)),
            dma((2, CHUNKS, NM - 1)),
            dma((2, 12)),
            dma((2, DP - 1)),
        ],
        compiler_params=pltpu.CompilerParams(
            collective_id=0, has_side_effects=True, vmem_limit_bytes=40 * 1024 * 1024
        ),
        name="monarch_layer",
    )(*(pltpu.with_memory_space_constraint(v, pltpu.HBM) for v in args))
    return store(results)


def solution(mesh):
    placed = (P("dp", "mp"), P("dp", "mp"), P("mp", "dp", None), P("mp", "dp", None))
    return jax.shard_map(
        on_device, mesh=mesh, in_specs=placed, out_specs=placed, check_vma=False
    )
```

```python
import functools
import math

import jax
import jax.numpy as jnp
from jax import lax
from jax.experimental import pallas as pl
from jax.experimental.pallas import tpu as pltpu
from jax.sharding import PartitionSpec as P

BLK = 256
LOC = 4
ROWS = 4
NZ, NH, NX = 8, 2, 4
DP = NZ * NH * NX
NY, NC = 4, 2
NM = NY * NC
FEAT = LOC * BLK
CHUNKS = 4
HALF = NZ // 2
BF, F32 = jnp.bfloat16, jnp.float32
MESH = pl.DeviceIdType.MESH


def dp_of(z, h, x):
    return (z * NH + h) * NX + x


def nn(a, b):
    return lax.dot_general(a, b, (((1,), (0,)), ((), ())), preferred_element_type=F32)


def nt(a, b):
    return lax.dot_general(a, b, (((1,), (1,)), ((), ())), preferred_element_type=F32)


def tn(a, b):
    return lax.dot_general(a, b, (((0,), (0,)), ((), ())), preferred_element_type=F32)


def natural_of_send(s):
    return ((s >> 5) & 3) * 128 + (s >> 7) * 32 + (s & 31)


def arrived_of_sorted(v):
    j, x, oo, h, b = v >> 8, (v >> 6) & 3, (v >> 3) & 7, (v >> 2) & 1, v & 3
    return (h * 4 + x) * 128 + b * 32 + j * 8 + oo


def natural_of_gathered(p):
    return ((p >> 2) & 3) * 256 + ((p >> 4) & 15) * 16 + (p >> 8) * 4 + (p & 3)


def sorted_of_gathered(p):
    return ((p >> 2) & 3) * 256 + (p >> 8) * 64 + ((p >> 4) & 15) * 4 + (p & 3)


def natural_of_sorted(s):
    return ((s >> 2) & 15) * 16 + (s >> 6) * 4 + (s & 3)


def write_perm(ref, source_of):
    rows, cols = ref.shape
    source = source_of(lax.broadcasted_iota(jnp.int32, (1, cols), 1))

    @pl.loop(0, rows // 128)
    def _(k):
        at = pl.ds(pl.multiple_of(k * 128, 128), 128)
        row = lax.broadcasted_iota(jnp.int32, (128, cols), 0) + k * 128
        ref[at, :] = jnp.where(row == source, 1.0, 0.0).astype(BF)


def kernel(
    scale, x_hbm, up_hbm, first_hbm, second_hbm,
    mixed_ref, gtok_ref, gfirst_ref, gsecond_ref,
    x_ref, up_ref, shard, buf_a, buf_b, w1, w2, xs, p_send, p_sort, p_nat, p_srt, p_x,
    u_tmp, send_a, recv_a, send_b, recv_b,
    g, s1, r1, s2, r2, t, s3, r3, s4, r4, s5, r5,
    lsem, gsem, sem_a, sem_b, rsem, fsem,
):
    me, mp = lax.axis_index("dp"), lax.axis_index("mp")
    z, h, x = me // (NH * NX), (me // NX) % NH, me % NX
    near, far, opp = x + 1 - 2 * (x % 2), NX - 1 - x, (x + 2) % NX
    yl, core = mp // NC, mp % NC
    ys = (yl, yl + 1 - 2 * (yl % 2), NY - 1 - yl, (yl + 2) % NY)
    end = ((yl + 1) // 2 + 1) % 2
    turns = [(3 * end + 2 * (1 - end), ys[2] * end + ys[3] * (1 - end)), (2 * end + 3 * (1 - end), ys[3] * end + ys[2] * (1 - end)), (1, ys[1])]
    kinds, mates = [], []
    for kind, row in turns:
        kinds += [2 * kind - 1, 2 * kind]
        mates += [row * NC + core, row * NC + 1 - core]
    kinds.append(0)
    mates.append(yl * NC + 1 - core)
    to_y, to_near, to_far = dp_of(z, 1 - h, x), dp_of(z, h, near), dp_of(z, h, far)
    to_z = [dp_of((z + k) % NZ, h, x) for k in range(1, NZ)]
    tc = x_ref.shape[0] // CHUNKS

    def push(src, dst, sems, k, peer):
        return pltpu.make_async_remote_copy(
            src_ref=src, dst_ref=dst, send_sem=sems.at[0, k], recv_sem=sems.at[1, k],
            device_id={"dp": peer}, device_id_type=MESH,
        )

    def swap(src, dst, sems, c, k):
        return pltpu.make_async_remote_copy(
            src_ref=src, dst_ref=dst,
            send_sem=sems.at[0, c, kinds[k]], recv_sem=sems.at[1, c, kinds[k]],
            device_id={"mp": mates[k]}, device_id_type=MESH,
        )

    bufs = (buf_a.at[0], buf_a.at[1], buf_b)
    sides = (1 - yl // 2, yl // 2)

    def gather_h(f):
        part = bufs[f].at[x, z, h]
        return push(part, part, gsem.at[f], 0, to_y)

    def gather_z(f):
        part = bufs[f].at[x, z]
        return [push(part, part, gsem.at[f], k, to_z[k - 1]) for k in range(1, NZ)]

    def gather_x(f):
        halves = [pl.ds(0, HALF), pl.ds(HALF, HALF)]

        def one(slot, half, k, peer):
            part = bufs[f].at[slot, halves[half]]
            return push(part, part, gsem.at[f], k, peer)

        def first():
            return [one(x, 0, 8, to_near), one(x, 1, 9, to_far)]

        def second():
            return [one(x, 1, 10, to_near), one(x, 0, 11, to_far)]

        def relay():
            return [one(near, 0, 12, to_far), one(far, 1, 13, to_near)]

        return first, second, relay

    def open_x(f):
        first, second, _ = gather_x(f)
        start(first() + second())

    def relay_x(f):
        first, _, relay = gather_x(f)
        for c, onward in zip(first(), relay()):
            c.wait_recv()
            onward.start()

    def close_x(f):
        first, second, relay = gather_x(f)
        rest = second() + relay()
        for c in rest:
            c.wait_recv()
        for c in first() + rest:
            c.wait_send()

    def start(copies):
        for c in copies:
            c.start()

    def wait(copies):
        for c in copies:
            c.wait()

    barrier = pltpu.get_barrier_semaphore()
    for peer in [to_y, to_near, to_far] + to_z:
        pl.semaphore_signal(barrier, inc=1, device_id={"dp": peer}, device_id_type=MESH)
    for mate in mates:
        pl.semaphore_signal(barrier, inc=1, device_id={"mp": mate}, device_id_type=MESH)
    load_x = pltpu.make_async_copy(x_hbm, x_ref, lsem.at[0])
    load_up = pltpu.make_async_copy(up_hbm, up_ref, lsem.at[1])
    load_rows = [
        pltpu.make_async_copy(ref, shard.at[f], lsem.at[2 + f])
        for f, ref in enumerate((first_hbm, second_hbm))
    ]
    start(load_rows)
    load_x.start()
    load_up.start()
    wait(load_rows)
    for f in range(2):
        rows = [shard[f, b].astype(F32) for b in range(LOC)]
        rows = jnp.concatenate(rows, axis=0)
        if f == 1:
            buf_b[x, z, h] = rows.astype(BF)
        else:
            low, high = rows[:, :128], rows[:, 128:]
            buf_a[0, x, z, h] = jnp.where(yl < NY // 2, high, low).astype(BF)
            buf_a[1, x, z, h] = jnp.where(yl < NY // 2, low, high).astype(BF)
    pl.semaphore_wait(barrier, 3 + len(to_z) + len(mates))
    for f in range(3):
        gather_h(f).start()
    write_perm(p_x, natural_of_sorted)
    for f in range(3):
        gather_h(f).wait()
        start(gather_z(f))
    write_perm(p_nat, natural_of_gathered)
    write_perm(p_send, natural_of_send)
    wait(gather_z(0))
    open_x(0)
    wait(gather_z(1))
    write_perm(p_sort, arrived_of_sorted)
    relay_x(0)
    open_x(1)
    write_perm(p_srt, sorted_of_gathered)
    g[...] = jnp.zeros_like(g)
    load_x.wait()
    close_x(0)

    def side_lanes(p):
        return pl.ds(pl.multiple_of(sides[p] * 128, 128), 128)

    def sort_first(p):
        rows = buf_a[p].reshape(FEAT, 128)
        for b in range(LOC):
            w1[b, :, side_lanes(p)] = nn(p_nat[b * BLK : (b + 1) * BLK, :], rows).astype(BF)

    def chunk(c):
        return pl.ds(pl.multiple_of(c * tc, tc), tc)

    def block(b):
        return slice(b * BLK, (b + 1) * BLK)

    def launch(send, recv, sems, c, ks):
        for k in ks:
            swap(send.at[c, mates[k]], recv.at[c, mp], sems, c, k).start()

    def launch_all(send, recv, sems, c):
        launch(send, recv, sems, c, range(NM - 1))
        recv[c, mp] = send[c, mp]

    def collect(recv, send, sems, c):
        for k in range(NM - 1):
            swap(send.at[c, mates[k]], recv.at[c, mates[k]], sems, c, k).wait_recv()
        return jnp.concatenate([recv[c, n] for n in range(NM)], axis=1)

    def send_side(half, side, c):
        lanes = nn(half, p_send[...]).astype(BF)
        for n in range(NM // 2):
            send_a[c, side * (NM // 2) + n] = lanes[:, n * 128 : (n + 1) * 128]

    for p in range(2):
        if p == 1:
            relay_x(1)
            wait(gather_z(2))
            open_x(2)
            close_x(1)
        sort_first(p)
        at = chunk(0)
        half = [nn(x_ref[at, block(b)], w1[b, :, side_lanes(p)]).astype(BF) for b in range(LOC)]
        send_side(jnp.concatenate(half, axis=1), sides[p], 0)
        launch(send_a, recv_a, sem_a, 0, (range(4), range(4, NM - 1))[p])
    recv_a[0, mp] = send_a[0, mp]

    def sort_tokens(at):
        for b in range(LOC):
            xs[at, block(b)] = nn(x_ref[at, block(b)], p_x[...]).astype(BF)

    @pl.loop(1, CHUNKS)
    def _(c):
        at = chunk(c)
        for b in range(LOC):
            u_tmp[:, block(b)] = nn(x_ref[at, block(b)], w1[b]).astype(BF)
        for side in range(2):
            half = [u_tmp[:, b * BLK + side * 128 : b * BLK + side * 128 + 128] for b in range(LOC)]
            send_side(jnp.concatenate(half, axis=1), side, c)
        launch_all(send_a, recv_a, sem_a, c)

        @pl.when(c == 1)
        def _():
            relay_x(2)

        sort_tokens(at)

    sort_tokens(chunk(0))
    close_x(2)
    rows = buf_b[...].reshape(FEAT, BLK)
    for b in range(LOC):
        w2[b] = nn(p_srt[block(b), :], rows).astype(BF)
    load_up.wait()

    @pl.loop(0, CHUNKS)
    def _(c):
        at = chunk(c)
        arrived = collect(recv_a, send_a, sem_a, c)
        for j in range(LOC):
            v = nn(arrived, p_sort[:, block(j)]).astype(BF)
            y = nn(v, w2[j])
            cdf = 0.5 * (1.0 + lax.erf(y * math.sqrt(0.5)))
            mixed_ref[at, block(j)] = (x_ref[at, block(j)].astype(F32) + y * cdf).astype(BF)
            slope = cdf + y * (jnp.exp(-0.5 * y * y) * (1.0 / math.sqrt(2.0 * math.pi)))
            cot = (up_ref[at, block(j)].astype(F32) * slope).astype(BF)
            g[1, j] += tn(v, cot).reshape(NX, 2, 32, BLK)
            u_tmp[:, block(j)] = nt(cot, w2[j]).astype(BF)
        for k in range(LOC):
            lanes = nt(u_tmp[...], p_sort[block(k), :]).astype(BF)
            send_b[c, 2 * k] = lanes[:, :128]
            send_b[c, 2 * k + 1] = lanes[:, 128:]
        launch_all(send_b, recv_b, sem_b, c)

    peer = (to_near, to_far)

    def sum_x1(k):
        return push(s1.at[k], r1.at[k], rsem, k, peer[k])

    def sum_x2(k):
        return push(s2.at[k], r2.at[k], rsem, 2 + k, peer[1 - k])

    def sum_z():
        return [push(s3.at[(z + k) % NZ], r3.at[k - 1], rsem, 3 + k, to_z[k - 1]) for k in range(1, NZ)]

    def sum_h():
        return push(s4, r4, rsem, 11, to_y)

    def reduce_x1():
        for k in range(2):
            s1[k, 0] = g[1, :, (near, far)[k], k].astype(BF)
            s1[k, 1] = g[1, :, opp, k].astype(BF)
            sum_x1(k).start()

    def reduce_x2():
        for k in range(2):
            sum_x1(k).wait_recv()
            s2[k] = (g[1, :, (far, near)[k], k] + r1[k, 1].astype(F32)).astype(BF)
            sum_x2(k).start()

    def reduce_z():
        for k in range(2):
            sum_x2(k).wait_recv()
            part = g[1, :, x, k] + r1[k, 0].astype(F32) + r2[k].astype(F32)
            t[:, k * HALF : (k + 1) * HALF] = part.reshape(LOC, HALF, NH * ROWS, BLK)
        for k in range(NZ):
            s3[k] = t[:, k].reshape(LOC * NH * ROWS, BLK).astype(BF)
        start(sum_z())

    def reduce_h():
        total = t[:, z].reshape(LOC * NH * ROWS, BLK)
        copies = sum_z()
        for k in range(NZ - 1):
            copies[k].wait_recv()
            total = total + r3[k].astype(F32)
        total = total.reshape(LOC, NH * ROWS, BLK)
        s4[...] = jnp.where(h == 0, total[:, ROWS:], total[:, :ROWS])
        gsecond_ref[...] = jnp.where(h == 0, total[:, :ROWS], total[:, ROWS:])
        sum_h().start()

    def reduce_end():
        sum_h().wait_recv()
        gsecond_ref[...] = (gsecond_ref[...] + r4[...]) * scale
        for k in range(2):
            sum_x1(k).wait_send()
            sum_x2(k).wait_send()
        for c in sum_z():
            c.wait_send()
        sum_h().wait_send()

    def final(to, slot):
        return pltpu.make_async_remote_copy(
            src_ref=s5.at[to], dst_ref=r5.at[slot],
            send_sem=fsem.at[0, to], recv_sem=fsem.at[1, slot],
            device_id={"dp": to}, device_id_type=MESH,
        )

    def send_final(hh):
        low = lax.broadcasted_iota(jnp.int32, (NZ, NH * ROWS, BLK), 1) < ROWS
        for xx in range(NX):
            pair = []
            for b in (0, 2):
                one, two = (g[0, b + k, xx].reshape(NZ, NH * ROWS, BLK) for k in range(2))
                if hh == 0:
                    pair.append(jnp.where(low, one, pltpu.roll(two, ROWS, 1)))
                else:
                    pair.append(jnp.where(low, pltpu.roll(one, ROWS, 1), two))
            rows = jnp.concatenate(pair, axis=1).astype(BF)
            for zz in range(NZ):
                s5[dp_of(zz, hh, xx)] = rows[zz]

            @pl.loop(0, NZ)
            def _(zz):
                to = dp_of(zz, hh, xx)
                pl.when(to != me)(lambda: final(to, me).start())

    reduce_x1()

    def first_grad(c):
        at = chunk(c)
        arrived = collect(recv_b, send_b, sem_b, c)
        side = [nt(arrived[:, k * 512 : (k + 1) * 512], p_send[...]).astype(BF) for k in range(2)]
        for b in range(LOC):
            du = jnp.concatenate([v[:, b * 128 : (b + 1) * 128] for v in side], axis=1)
            u_tmp[:, block(b)] = du
            g[0, b] += tn(xs[at, block(b)], du).reshape(NX, 2, 32, BLK)

    def token_grad(c):
        at = chunk(c)
        for b in range(LOC):
            back = nt(u_tmp[:, block(b)], w1[b])
            gtok_ref[at, block(b)] = (up_ref[at, block(b)].astype(F32) + back).astype(BF)

    @pl.loop(0, CHUNKS - 1)
    def _(c):
        first_grad(c)
        token_grad(c)
        for step, run in enumerate((reduce_x2, reduce_z, reduce_h)):
            pl.when(c == step)(run)

    first_grad(CHUNKS - 1)
    for hh in range(NH):

        @pl.when(h == hh)
        def _():
            send_final(1 - hh)
            send_final(hh)

    token_grad(CHUNKS - 1)
    reduce_end()

    @pl.loop(0, CHUNKS)
    def _(c):
        for k in range(NM - 1):
            swap(send_a.at[c, mates[k]], recv_a.at[c, mp], sem_a, c, k).wait_send()
            swap(send_b.at[c, mates[k]], recv_b.at[c, mp], sem_b, c, k).wait_send()

    def add_final(i, total):
        peer = (me + i) % DP
        final(peer, peer).wait_recv()
        return total + r5[peer].astype(F32)

    total = lax.fori_loop(1, DP, add_final, s5[me].astype(F32)) * scale
    for b in range(LOC):
        gfirst_ref[b] = total[b * ROWS : (b + 1) * ROWS]

    @pl.loop(1, DP)
    def _(i):
        peer = (me + i) % DP
        final(peer, peer).wait_send()


def store_kernel(*refs):
    count = len(refs) // 2
    sems = refs[-1]
    copies = [
        pltpu.make_async_copy(refs[i], refs[count + i], sems.at[i]) for i in range(count)
    ]
    for c in copies:
        c.start()
    for c in copies:
        c.wait()


def store(results):
    count = len(results)
    return pl.pallas_call(
        store_kernel,
        out_shape=tuple(jax.ShapeDtypeStruct(r.shape, r.dtype) for r in results),
        in_specs=[pl.BlockSpec(memory_space=pltpu.VMEM)] * count,
        out_specs=(pl.BlockSpec(memory_space=pltpu.HBM),) * count,
        scratch_shapes=[pltpu.SemaphoreType.DMA((count,))],
        name="store_results",
    )(*(pltpu.with_memory_space_constraint(r, pltpu.VMEM) for r in results))


def on_device(*args):
    tok = args[0].shape[0]
    tc = tok // CHUNKS
    scale = 1.0 / math.sqrt(tok * lax.axis_size("dp"))
    vmem = pl.BlockSpec(memory_space=pltpu.VMEM)
    hbm = pl.BlockSpec(memory_space=pltpu.HBM)
    dma = pltpu.SemaphoreType.DMA
    slot = NH * ROWS
    results = pl.pallas_call(
        functools.partial(kernel, scale),
        out_shape=(
            jax.ShapeDtypeStruct((tok, FEAT), BF),
            jax.ShapeDtypeStruct((tok, FEAT), BF),
            jax.ShapeDtypeStruct((LOC, ROWS, BLK), F32),
            jax.ShapeDtypeStruct((LOC, ROWS, BLK), F32),
        ),
        in_specs=[hbm] * 4,
        out_specs=(vmem,) * 4,
        scratch_shapes=[
            pltpu.VMEM((tok, FEAT), BF),
            pltpu.VMEM((tok, FEAT), BF),
            pltpu.VMEM((2, LOC, ROWS, BLK), BF),
            pltpu.VMEM((2, NX, NZ, NH, LOC * ROWS, 128), BF),
            pltpu.VMEM((NX, NZ, NH, LOC * ROWS, BLK), BF),
            pltpu.VMEM((LOC, BLK, BLK), BF),
            pltpu.VMEM((LOC, BLK, BLK), BF),
            pltpu.VMEM((tok, FEAT), BF),
            pltpu.VMEM((FEAT // 2, FEAT // 2), BF),
            pltpu.VMEM((FEAT, FEAT), BF),
            pltpu.VMEM((FEAT, FEAT), BF),
            pltpu.VMEM((FEAT, FEAT), BF),
            pltpu.VMEM((BLK, BLK), BF),
            pltpu.VMEM((tc, FEAT), BF),
            pltpu.VMEM((CHUNKS, NM, tc, 128), BF),
            pltpu.VMEM((CHUNKS, NM, tc, 128), BF),
            pltpu.VMEM((CHUNKS, NM, tc, 128), BF),
            pltpu.VMEM((CHUNKS, NM, tc, 128), BF),
            pltpu.VMEM((2, LOC, NX, 2, HALF * slot, BLK), F32),
            pltpu.VMEM((2, 2, LOC, HALF * slot, BLK), BF),
            pltpu.VMEM((2, 2, LOC, HALF * slot, BLK), BF),
            pltpu.VMEM((2, LOC, HALF * slot, BLK), BF),
            pltpu.VMEM((2, LOC, HALF * slot, BLK), BF),
            pltpu.VMEM((LOC, NZ, slot, BLK), F32),
            pltpu.VMEM((NZ, LOC * slot, BLK), BF),
            pltpu.VMEM((NZ - 1, LOC * slot, BLK), BF),
            pltpu.VMEM((LOC, ROWS, BLK), F32),
            pltpu.VMEM((LOC, ROWS, BLK), F32),
            pltpu.VMEM((DP, LOC * ROWS, BLK), BF),
            pltpu.VMEM((DP, LOC * ROWS, BLK), BF),
            dma((4,)),
            dma((3, 2, 14)),
            dma((2, CHUNKS, NM - 1)),
            dma((2, CHUNKS, NM - 1)),
            dma((2, 12)),
            dma((2, DP)),
        ],
        compiler_params=pltpu.CompilerParams(
            collective_id=0, has_side_effects=True, vmem_limit_bytes=40 * 1024 * 1024
        ),
        name="monarch_layer",
    )(*(pltpu.with_memory_space_constraint(v, pltpu.HBM) for v in args))
    return store(results)


def solution(mesh):
    placed = (P("dp", "mp"), P("dp", "mp"), P("mp", "dp", None), P("mp", "dp", None))
    return jax.shard_map(
        on_device, mesh=mesh, in_specs=placed, out_specs=placed, check_vma=False
    )
```

```python
import functools
import math

import jax
import jax.numpy as jnp
from jax import lax
from jax.experimental import pallas as pl
from jax.experimental.pallas import tpu as pltpu
from jax.sharding import PartitionSpec as P

BLK = 256
LOC = 4
ROWS = 4
NZ, NH, NX = 8, 2, 4
DP = NZ * NH * NX
NY, NC = 4, 2
NM = NY * NC
FEAT = LOC * BLK
CHUNKS = 4
HALF = NZ // 2
BF, F32 = jnp.bfloat16, jnp.float32
MESH = pl.DeviceIdType.MESH


def dp_of(z, h, x):
    return (z * NH + h) * NX + x


def nn(a, b):
    return lax.dot_general(a, b, (((1,), (0,)), ((), ())), preferred_element_type=F32)


def nt(a, b):
    return lax.dot_general(a, b, (((1,), (1,)), ((), ())), preferred_element_type=F32)


def tn(a, b):
    return lax.dot_general(a, b, (((0,), (0,)), ((), ())), preferred_element_type=F32)


def natural_of_send(s):
    return ((s >> 5) & 3) * 128 + (s >> 7) * 32 + (s & 31)


def arrived_of_sorted(v):
    j, x, oo, h, b = v >> 8, (v >> 6) & 3, (v >> 3) & 7, (v >> 2) & 1, v & 3
    return (h * 4 + x) * 128 + b * 32 + j * 8 + oo


def natural_of_gathered(p):
    return ((p >> 2) & 3) * 256 + ((p >> 4) & 15) * 16 + (p >> 8) * 4 + (p & 3)


def sorted_of_gathered(p):
    return ((p >> 2) & 3) * 256 + (p >> 8) * 64 + ((p >> 4) & 15) * 4 + (p & 3)


def natural_of_sorted(s):
    return ((s >> 2) & 15) * 16 + (s >> 6) * 4 + (s & 3)


def write_perm(ref, source_of):
    rows, cols = ref.shape
    source = source_of(lax.broadcasted_iota(jnp.int32, (1, cols), 1))

    @pl.loop(0, rows // 128)
    def _(k):
        at = pl.ds(pl.multiple_of(k * 128, 128), 128)
        row = lax.broadcasted_iota(jnp.int32, (128, cols), 0) + k * 128
        ref[at, :] = jnp.where(row == source, 1.0, 0.0).astype(BF)


def kernel(
    scale, x_hbm, up_hbm, first_hbm, second_hbm,
    mixed_ref, gtok_ref, gfirst_ref, gsecond_ref,
    x_ref, up_ref, shard, buf_a, buf_b, w1, w2, xs, p_send, p_sort, p_nat, p_srt, p_x,
    u_tmp, send_a, recv_a, send_b, recv_b,
    g, s1, r1, s2, r2, t, s3, r3, s4, r4, s5, rx, s6, r6, r5,
    lsem, gsem, sem_a, sem_b, rsem, fsem, xsem, zsem,
):
    me, mp = lax.axis_index("dp"), lax.axis_index("mp")
    z, h, x = me // (NH * NX), (me // NX) % NH, me % NX
    near, far, opp = x + 1 - 2 * (x % 2), NX - 1 - x, (x + 2) % NX
    yl, core = mp // NC, mp % NC
    ys = (yl, yl + 1 - 2 * (yl % 2), NY - 1 - yl, (yl + 2) % NY)
    end = ((yl + 1) // 2 + 1) % 2
    turns = [(3 * end + 2 * (1 - end), ys[2] * end + ys[3] * (1 - end)), (2 * end + 3 * (1 - end), ys[3] * end + ys[2] * (1 - end)), (1, ys[1])]
    kinds, mates = [], []
    for kind, row in turns:
        kinds += [2 * kind - 1, 2 * kind]
        mates += [row * NC + core, row * NC + 1 - core]
    kinds.append(0)
    mates.append(yl * NC + 1 - core)
    to_y, to_near, to_far = dp_of(z, 1 - h, x), dp_of(z, h, near), dp_of(z, h, far)
    to_z = [dp_of((z + k) % NZ, h, x) for k in range(1, NZ)]
    tc = x_ref.shape[0] // CHUNKS

    def push(src, dst, sems, k, peer):
        return pltpu.make_async_remote_copy(
            src_ref=src, dst_ref=dst, send_sem=sems.at[0, k], recv_sem=sems.at[1, k],
            device_id={"dp": peer}, device_id_type=MESH,
        )

    def swap(src, dst, sems, c, k):
        return pltpu.make_async_remote_copy(
            src_ref=src, dst_ref=dst,
            send_sem=sems.at[0, c, kinds[k]], recv_sem=sems.at[1, c, kinds[k]],
            device_id={"mp": mates[k]}, device_id_type=MESH,
        )

    bufs = (buf_a.at[0], buf_a.at[1], buf_b)
    sides = (1 - yl // 2, yl // 2)

    def gather_h(f):
        part = bufs[f].at[x, z, h]
        return push(part, part, gsem.at[f], 0, to_y)

    def gather_z(f):
        part = bufs[f].at[x, z]
        return [push(part, part, gsem.at[f], k, to_z[k - 1]) for k in range(1, NZ)]

    def gather_x(f):
        halves = [pl.ds(0, HALF), pl.ds(HALF, HALF)]

        def one(slot, half, k, peer):
            part = bufs[f].at[slot, halves[half]]
            return push(part, part, gsem.at[f], k, peer)

        def first():
            return [one(x, 0, 8, to_near), one(x, 1, 9, to_far)]

        def second():
            return [one(x, 1, 10, to_near), one(x, 0, 11, to_far)]

        def relay():
            return [one(near, 0, 12, to_far), one(far, 1, 13, to_near)]

        return first, second, relay

    def open_x(f):
        first, second, _ = gather_x(f)
        start(first() + second())

    def relay_x(f):
        first, _, relay = gather_x(f)
        for c, onward in zip(first(), relay()):
            c.wait_recv()
            onward.start()

    def close_x(f):
        first, second, relay = gather_x(f)
        rest = second() + relay()
        for c in rest:
            c.wait_recv()
        for c in first() + rest:
            c.wait_send()

    def start(copies):
        for c in copies:
            c.start()

    def wait(copies):
        for c in copies:
            c.wait()

    barrier = pltpu.get_barrier_semaphore()
    for peer in [to_y, to_near, to_far] + to_z:
        pl.semaphore_signal(barrier, inc=1, device_id={"dp": peer}, device_id_type=MESH)
    for mate in mates:
        pl.semaphore_signal(barrier, inc=1, device_id={"mp": mate}, device_id_type=MESH)
    load_x = pltpu.make_async_copy(x_hbm, x_ref, lsem.at[0])
    load_up = pltpu.make_async_copy(up_hbm, up_ref, lsem.at[1])
    load_rows = [
        pltpu.make_async_copy(ref, shard.at[f], lsem.at[2 + f])
        for f, ref in enumerate((first_hbm, second_hbm))
    ]
    start(load_rows)
    load_x.start()
    load_up.start()
    wait(load_rows)
    for f in range(2):
        rows = [shard[f, b].astype(F32) for b in range(LOC)]
        rows = jnp.concatenate(rows, axis=0)
        if f == 1:
            buf_b[x, z, h] = rows.astype(BF)
        else:
            low, high = rows[:, :128], rows[:, 128:]
            buf_a[0, x, z, h] = jnp.where(yl < NY // 2, high, low).astype(BF)
            buf_a[1, x, z, h] = jnp.where(yl < NY // 2, low, high).astype(BF)
    pl.semaphore_wait(barrier, 3 + len(to_z) + len(mates))
    for f in range(3):
        gather_h(f).start()
    write_perm(p_x, natural_of_sorted)
    for f in range(3):
        gather_h(f).wait()
        start(gather_z(f))
    write_perm(p_nat, natural_of_gathered)
    write_perm(p_send, natural_of_send)
    wait(gather_z(0))
    open_x(0)
    wait(gather_z(1))
    write_perm(p_sort, arrived_of_sorted)
    relay_x(0)
    open_x(1)
    write_perm(p_srt, sorted_of_gathered)
    g[...] = jnp.zeros_like(g)
    load_x.wait()
    close_x(0)

    def side_lanes(p):
        return pl.ds(pl.multiple_of(sides[p] * 128, 128), 128)

    def sort_first(p):
        rows = buf_a[p].reshape(FEAT, 128)
        for b in range(LOC):
            w1[b, :, side_lanes(p)] = nn(p_nat[b * BLK : (b + 1) * BLK, :], rows).astype(BF)

    def chunk(c):
        return pl.ds(pl.multiple_of(c * tc, tc), tc)

    def block(b):
        return slice(b * BLK, (b + 1) * BLK)

    def launch(send, recv, sems, c, ks):
        for k in ks:
            swap(send.at[c, mates[k]], recv.at[c, mp], sems, c, k).start()

    def launch_all(send, recv, sems, c):
        launch(send, recv, sems, c, range(NM - 1))
        recv[c, mp] = send[c, mp]

    def collect(recv, send, sems, c):
        for k in range(NM - 1):
            swap(send.at[c, mates[k]], recv.at[c, mates[k]], sems, c, k).wait_recv()
        return jnp.concatenate([recv[c, n] for n in range(NM)], axis=1)

    def send_side(half, side, c):
        lanes = nn(half, p_send[...]).astype(BF)
        for n in range(NM // 2):
            send_a[c, side * (NM // 2) + n] = lanes[:, n * 128 : (n + 1) * 128]

    for p in range(2):
        if p == 1:
            relay_x(1)
            wait(gather_z(2))
            open_x(2)
            close_x(1)
        sort_first(p)
        at = chunk(0)
        half = [nn(x_ref[at, block(b)], w1[b, :, side_lanes(p)]).astype(BF) for b in range(LOC)]
        send_side(jnp.concatenate(half, axis=1), sides[p], 0)
        launch(send_a, recv_a, sem_a, 0, (range(4), range(4, NM - 1))[p])
    recv_a[0, mp] = send_a[0, mp]

    def sort_tokens(at):
        for b in range(LOC):
            xs[at, block(b)] = nn(x_ref[at, block(b)], p_x[...]).astype(BF)

    @pl.loop(1, CHUNKS)
    def _(c):
        at = chunk(c)
        for b in range(LOC):
            u_tmp[:, block(b)] = nn(x_ref[at, block(b)], w1[b]).astype(BF)
        for side in range(2):
            half = [u_tmp[:, b * BLK + side * 128 : b * BLK + side * 128 + 128] for b in range(LOC)]
            send_side(jnp.concatenate(half, axis=1), side, c)
        launch_all(send_a, recv_a, sem_a, c)

        @pl.when(c == 1)
        def _():
            relay_x(2)

        sort_tokens(at)

    sort_tokens(chunk(0))
    close_x(2)
    rows = buf_b[...].reshape(FEAT, BLK)
    for b in range(LOC):
        w2[b] = nn(p_srt[block(b), :], rows).astype(BF)
    load_up.wait()

    @pl.loop(0, CHUNKS)
    def _(c):
        at = chunk(c)
        arrived = collect(recv_a, send_a, sem_a, c)
        for j in range(LOC):
            v = nn(arrived, p_sort[:, block(j)]).astype(BF)
            y = nn(v, w2[j])
            cdf = 0.5 * (1.0 + lax.erf(y * math.sqrt(0.5)))
            mixed_ref[at, block(j)] = (x_ref[at, block(j)].astype(F32) + y * cdf).astype(BF)
            slope = cdf + y * (jnp.exp(-0.5 * y * y) * (1.0 / math.sqrt(2.0 * math.pi)))
            cot = (up_ref[at, block(j)].astype(F32) * slope).astype(BF)
            g[1, j] += tn(v, cot).reshape(NX, 2, 32, BLK)
            u_tmp[:, block(j)] = nt(cot, w2[j]).astype(BF)
        for k in range(LOC):
            lanes = nt(u_tmp[...], p_sort[block(k), :]).astype(BF)
            send_b[c, 2 * k] = lanes[:, :128]
            send_b[c, 2 * k + 1] = lanes[:, 128:]
        launch_all(send_b, recv_b, sem_b, c)

    peer = (to_near, to_far)

    def sum_x1(k):
        return push(s1.at[k], r1.at[k], rsem, k, peer[k])

    def sum_x2(k):
        return push(s2.at[k], r2.at[k], rsem, 2 + k, peer[1 - k])

    def sum_z():
        return [push(s3.at[(z + k) % NZ], r3.at[k - 1], rsem, 3 + k, to_z[k - 1]) for k in range(1, NZ)]

    def sum_h():
        return push(s4, r4, rsem, 11, to_y)

    def reduce_x1():
        for k in range(2):
            s1[k, 0] = g[1, :, (near, far)[k], k].astype(BF)
            s1[k, 1] = g[1, :, opp, k].astype(BF)
            sum_x1(k).start()

    def reduce_x2():
        for k in range(2):
            sum_x1(k).wait_recv()
            s2[k] = (g[1, :, (far, near)[k], k] + r1[k, 1].astype(F32)).astype(BF)
            sum_x2(k).start()

    def reduce_z():
        for k in range(2):
            sum_x2(k).wait_recv()
            part = g[1, :, x, k] + r1[k, 0].astype(F32) + r2[k].astype(F32)
            t[:, k * HALF : (k + 1) * HALF] = part.reshape(LOC, HALF, NH * ROWS, BLK)
        for k in range(NZ):
            s3[k] = t[:, k].reshape(LOC * NH * ROWS, BLK).astype(BF)
        start(sum_z())

    def reduce_h():
        total = t[:, z].reshape(LOC * NH * ROWS, BLK)
        copies = sum_z()
        for k in range(NZ - 1):
            copies[k].wait_recv()
            total = total + r3[k].astype(F32)
        total = total.reshape(LOC, NH * ROWS, BLK)
        s4[...] = jnp.where(h == 0, total[:, ROWS:], total[:, :ROWS])
        gsecond_ref[...] = jnp.where(h == 0, total[:, :ROWS], total[:, ROWS:])
        sum_h().start()

    def reduce_end():
        sum_h().wait_recv()
        gsecond_ref[...] = (gsecond_ref[...] + r4[...]) * scale
        for k in range(2):
            sum_x1(k).wait_send()
            sum_x2(k).wait_send()
        for c in sum_z():
            c.wait_send()
        sum_h().wait_send()

    def rows_copy(src, dst, sems, out_slot, in_slot, to):
        return pltpu.make_async_remote_copy(
            src_ref=src, dst_ref=dst, send_sem=sems.at[0, out_slot], recv_sem=sems.at[1, in_slot],
            device_id={"dp": to}, device_id_type=MESH,
        )

    def cross_x(to, slot):
        return rows_copy(s5.at[0, to], rx.at[slot], xsem, to, slot, dp_of(z, h, to))

    def cross_z(to, slot):
        return rows_copy(s6.at[to], r6.at[slot], zsem, to, slot, dp_of(to, 1 - h, x))

    def same(to, slot):
        return rows_copy(
            s5.at[1, to // NZ, to % NZ], r5.at[slot], fsem, to, slot, dp_of(to % NZ, h, to // NZ)
        )

    spot = x * NZ + z

    def send_final(side, hh):
        low = lax.broadcasted_iota(jnp.int32, (NZ, NH * ROWS, BLK), 1) < ROWS
        for xx in range(NX):
            pair = []
            for b in (0, 2):
                one, two = (g[0, b + k, xx].reshape(NZ, NH * ROWS, BLK) for k in range(2))
                if hh == 0:
                    pair.append(jnp.where(low, one, pltpu.roll(two, ROWS, 1)))
                else:
                    pair.append(jnp.where(low, pltpu.roll(one, ROWS, 1), two))
            s5[side, xx] = jnp.concatenate(pair, axis=1).astype(BF)
            if side == 0:
                pl.when(x != xx)(lambda: cross_x(xx, x).start())
            else:

                @pl.loop(xx * NZ, (xx + 1) * NZ)
                def _(to):
                    pl.when(to != spot)(lambda: same(to, spot).start())

    def cross_final():
        acc = s5[0, x].astype(F32)
        for k in (near, far, opp):
            cross_x(k, k).wait_recv()
            acc = acc + rx[k].astype(F32)
        s6[...] = acc.astype(BF)

        @pl.loop(0, NZ)
        def _(to):
            cross_z(to, z).start()

    reduce_x1()

    def first_grad(c):
        at = chunk(c)
        arrived = collect(recv_b, send_b, sem_b, c)
        side = [nt(arrived[:, k * 512 : (k + 1) * 512], p_send[...]).astype(BF) for k in range(2)]
        for b in range(LOC):
            du = jnp.concatenate([v[:, b * 128 : (b + 1) * 128] for v in side], axis=1)
            u_tmp[:, block(b)] = du
            g[0, b] += tn(xs[at, block(b)], du).reshape(NX, 2, 32, BLK)

    def token_grad(c):
        at = chunk(c)
        for b in range(LOC):
            back = nt(u_tmp[:, block(b)], w1[b])
            gtok_ref[at, block(b)] = (up_ref[at, block(b)].astype(F32) + back).astype(BF)

    @pl.loop(0, CHUNKS - 1)
    def _(c):
        first_grad(c)
        token_grad(c)
        for step, run in enumerate((reduce_x2, reduce_z, reduce_h)):
            pl.when(c == step)(run)

    first_grad(CHUNKS - 1)
    for hh in range(NH):

        @pl.when(h == hh)
        def _():
            send_final(0, 1 - hh)
            send_final(1, hh)

    token_grad(CHUNKS - 1)
    cross_final()
    reduce_end()

    @pl.loop(0, CHUNKS)
    def _(c):
        for k in range(NM - 1):
            swap(send_a.at[c, mates[k]], recv_a.at[c, mp], sem_a, c, k).wait_send()
            swap(send_b.at[c, mates[k]], recv_b.at[c, mp], sem_b, c, k).wait_send()

    def add_same(i, total):
        peer = (spot + i) % (NX * NZ)
        same(peer, peer).wait_recv()
        return total + r5[peer].astype(F32)

    def add_cross(i, total):
        cross_z(i, i).wait_recv()
        return total + r6[i].astype(F32)

    total = lax.fori_loop(1, NX * NZ, add_same, s5[1, x, z].astype(F32))
    total = lax.fori_loop(0, NZ, add_cross, total) * scale
    for b in range(LOC):
        gfirst_ref[b] = total[b * ROWS : (b + 1) * ROWS]

    for k in (near, far, opp):
        cross_x(k, k).wait_send()

    @pl.loop(0, NZ)
    def _(i):
        cross_z(i, i).wait_send()

    @pl.loop(1, NX * NZ)
    def _(i):
        peer = (spot + i) % (NX * NZ)
        same(peer, peer).wait_send()


def store_kernel(*refs):
    count = len(refs) // 2
    sems = refs[-1]
    copies = [
        pltpu.make_async_copy(refs[i], refs[count + i], sems.at[i]) for i in range(count)
    ]
    for c in copies:
        c.start()
    for c in copies:
        c.wait()


def store(results):
    count = len(results)
    return pl.pallas_call(
        store_kernel,
        out_shape=tuple(jax.ShapeDtypeStruct(r.shape, r.dtype) for r in results),
        in_specs=[pl.BlockSpec(memory_space=pltpu.VMEM)] * count,
        out_specs=(pl.BlockSpec(memory_space=pltpu.HBM),) * count,
        scratch_shapes=[pltpu.SemaphoreType.DMA((count,))],
        name="store_results",
    )(*(pltpu.with_memory_space_constraint(r, pltpu.VMEM) for r in results))


def on_device(*args):
    tok = args[0].shape[0]
    tc = tok // CHUNKS
    scale = 1.0 / math.sqrt(tok * lax.axis_size("dp"))
    vmem = pl.BlockSpec(memory_space=pltpu.VMEM)
    hbm = pl.BlockSpec(memory_space=pltpu.HBM)
    dma = pltpu.SemaphoreType.DMA
    slot = NH * ROWS
    results = pl.pallas_call(
        functools.partial(kernel, scale),
        out_shape=(
            jax.ShapeDtypeStruct((tok, FEAT), BF),
            jax.ShapeDtypeStruct((tok, FEAT), BF),
            jax.ShapeDtypeStruct((LOC, ROWS, BLK), F32),
            jax.ShapeDtypeStruct((LOC, ROWS, BLK), F32),
        ),
        in_specs=[hbm] * 4,
        out_specs=(vmem,) * 4,
        scratch_shapes=[
            pltpu.VMEM((tok, FEAT), BF),
            pltpu.VMEM((tok, FEAT), BF),
            pltpu.VMEM((2, LOC, ROWS, BLK), BF),
            pltpu.VMEM((2, NX, NZ, NH, LOC * ROWS, 128), BF),
            pltpu.VMEM((NX, NZ, NH, LOC * ROWS, BLK), BF),
            pltpu.VMEM((LOC, BLK, BLK), BF),
            pltpu.VMEM((LOC, BLK, BLK), BF),
            pltpu.VMEM((tok, FEAT), BF),
            pltpu.VMEM((FEAT // 2, FEAT // 2), BF),
            pltpu.VMEM((FEAT, FEAT), BF),
            pltpu.VMEM((FEAT, FEAT), BF),
            pltpu.VMEM((FEAT, FEAT), BF),
            pltpu.VMEM((BLK, BLK), BF),
            pltpu.VMEM((tc, FEAT), BF),
            pltpu.VMEM((CHUNKS, NM, tc, 128), BF),
            pltpu.VMEM((CHUNKS, NM, tc, 128), BF),
            pltpu.VMEM((CHUNKS, NM, tc, 128), BF),
            pltpu.VMEM((CHUNKS, NM, tc, 128), BF),
            pltpu.VMEM((2, LOC, NX, 2, HALF * slot, BLK), F32),
            pltpu.VMEM((2, 2, LOC, HALF * slot, BLK), BF),
            pltpu.VMEM((2, 2, LOC, HALF * slot, BLK), BF),
            pltpu.VMEM((2, LOC, HALF * slot, BLK), BF),
            pltpu.VMEM((2, LOC, HALF * slot, BLK), BF),
            pltpu.VMEM((LOC, NZ, slot, BLK), F32),
            pltpu.VMEM((NZ, LOC * slot, BLK), BF),
            pltpu.VMEM((NZ - 1, LOC * slot, BLK), BF),
            pltpu.VMEM((LOC, ROWS, BLK), F32),
            pltpu.VMEM((LOC, ROWS, BLK), F32),
            pltpu.VMEM((2, NX, NZ, LOC * ROWS, BLK), BF),
            pltpu.VMEM((NX, NZ, LOC * ROWS, BLK), BF),
            pltpu.VMEM((NZ, LOC * ROWS, BLK), BF),
            pltpu.VMEM((NZ, LOC * ROWS, BLK), BF),
            pltpu.VMEM((NX * NZ, LOC * ROWS, BLK), BF),
            dma((4,)),
            dma((3, 2, 14)),
            dma((2, CHUNKS, NM - 1)),
            dma((2, CHUNKS, NM - 1)),
            dma((2, 12)),
            dma((2, NX * NZ)),
            dma((2, NX)),
            dma((2, NZ)),
        ],
        compiler_params=pltpu.CompilerParams(
            collective_id=0, has_side_effects=True, vmem_limit_bytes=40 * 1024 * 1024
        ),
        name="monarch_layer",
    )(*(pltpu.with_memory_space_constraint(v, pltpu.HBM) for v in args))
    return store(results)


def solution(mesh):
    placed = (P("dp", "mp"), P("dp", "mp"), P("mp", "dp", None), P("mp", "dp", None))
    return jax.shard_map(
        on_device, mesh=mesh, in_specs=placed, out_specs=placed, check_vma=False
    )
```

```python
import functools
import math

import jax
import jax.numpy as jnp
from jax import lax
from jax.experimental import pallas as pl
from jax.experimental.pallas import tpu as pltpu
from jax.sharding import PartitionSpec as P

BLK = 256
LOC = 4
ROWS = 4
NZ, NH, NX = 8, 2, 4
DP = NZ * NH * NX
NY, NC = 4, 2
NM = NY * NC
FEAT = LOC * BLK
CHUNKS = 4
HALF = NZ // 2
BF, F32 = jnp.bfloat16, jnp.float32
MESH = pl.DeviceIdType.MESH


def dp_of(z, h, x):
    return (z * NH + h) * NX + x


def nn(a, b):
    return lax.dot_general(a, b, (((1,), (0,)), ((), ())), preferred_element_type=F32)


def nt(a, b):
    return lax.dot_general(a, b, (((1,), (1,)), ((), ())), preferred_element_type=F32)


def tn(a, b):
    return lax.dot_general(a, b, (((0,), (0,)), ((), ())), preferred_element_type=F32)


def natural_of_send(s):
    return ((s >> 5) & 3) * 128 + (s >> 7) * 32 + (s & 31)


def arrived_of_sorted(v):
    j, x, oo, h, b = v >> 8, (v >> 6) & 3, (v >> 3) & 7, (v >> 2) & 1, v & 3
    return (h * 4 + x) * 128 + b * 32 + j * 8 + oo


def natural_of_gathered(p):
    return ((p >> 2) & 3) * 256 + ((p >> 4) & 15) * 16 + (p >> 8) * 4 + (p & 3)


def sorted_of_gathered(p):
    return ((p >> 2) & 3) * 256 + (p >> 8) * 64 + ((p >> 4) & 15) * 4 + (p & 3)


def natural_of_sorted(s):
    return ((s >> 2) & 15) * 16 + (s >> 6) * 4 + (s & 3)


def write_perm(ref, source_of):
    rows, cols = ref.shape
    source = source_of(lax.broadcasted_iota(jnp.int32, (1, cols), 1))

    @pl.loop(0, rows // 128)
    def _(k):
        at = pl.ds(pl.multiple_of(k * 128, 128), 128)
        row = lax.broadcasted_iota(jnp.int32, (128, cols), 0) + k * 128
        ref[at, :] = jnp.where(row == source, 1.0, 0.0).astype(BF)


def kernel(
    scale, x_hbm, up_hbm, first_hbm, second_hbm,
    mixed_ref, gtok_ref, gfirst_ref, gsecond_ref,
    x_ref, up_ref, shard, buf_a, buf_b, w1, w2, xs, p_send, p_sort, p_nat, p_srt, p_x,
    u_tmp, send_a, recv_a, send_b, recv_b,
    g, s1, r1, s2, r2, t, s3, r3, s4, r4, s5, rx, s6, r6, r5,
    lsem, gsem, sem_a, sem_b, rsem, fsem, xsem, zsem,
):
    me, mp = lax.axis_index("dp"), lax.axis_index("mp")
    z, h, x = me // (NH * NX), (me // NX) % NH, me % NX
    near, far, opp = x + 1 - 2 * (x % 2), NX - 1 - x, (x + 2) % NX
    yl, core = mp // NC, mp % NC
    ys = (yl, yl + 1 - 2 * (yl % 2), NY - 1 - yl, (yl + 2) % NY)
    end = ((yl + 1) // 2 + 1) % 2
    turns = [(3 * end + 2 * (1 - end), ys[2] * end + ys[3] * (1 - end)), (2 * end + 3 * (1 - end), ys[3] * end + ys[2] * (1 - end)), (1, ys[1])]
    kinds, mates = [], []
    for kind, row in turns:
        kinds += [2 * kind - 1, 2 * kind]
        mates += [row * NC + core, row * NC + 1 - core]
    kinds.append(0)
    mates.append(yl * NC + 1 - core)
    to_y, to_near, to_far = dp_of(z, 1 - h, x), dp_of(z, h, near), dp_of(z, h, far)
    to_z = [dp_of((z + k) % NZ, h, x) for k in range(1, NZ)]
    tc = x_ref.shape[0] // CHUNKS

    def push(src, dst, sems, k, peer):
        return pltpu.make_async_remote_copy(
            src_ref=src, dst_ref=dst, send_sem=sems.at[0, k], recv_sem=sems.at[1, k],
            device_id={"dp": peer}, device_id_type=MESH,
        )

    def swap(src, dst, sems, c, k):
        return pltpu.make_async_remote_copy(
            src_ref=src, dst_ref=dst,
            send_sem=sems.at[0, c, kinds[k]], recv_sem=sems.at[1, c, kinds[k]],
            device_id={"mp": mates[k]}, device_id_type=MESH,
        )

    bufs = (buf_a.at[0], buf_a.at[1], buf_b)
    sides = (1 - yl // 2, yl // 2)

    def gather_h(f):
        part = bufs[f].at[x, z, h]
        return push(part, part, gsem.at[f], 0, to_y)

    runs = ((0, h, 0), (0, 1 - h, 14), (1, None, 0), (2, None, 0))

    def gather_z(run):
        f, hh, base = run
        part = bufs[f].at[x, z] if hh is None else bufs[f].at[x, z, hh]
        return [push(part, part, gsem.at[f], base + k, to_z[k - 1]) for k in range(1, NZ)]

    def gather_x(run):
        f, hh, base = run
        halves = [pl.ds(0, HALF), pl.ds(HALF, HALF)]

        def one(slot, half, k, peer):
            part = bufs[f].at[slot, halves[half]] if hh is None else bufs[f].at[slot, halves[half], hh]
            return push(part, part, gsem.at[f], base + k, peer)

        def first():
            return [one(x, 0, 8, to_near), one(x, 1, 9, to_far)]

        def second():
            return [one(x, 1, 10, to_near), one(x, 0, 11, to_far)]

        def relay():
            return [one(near, 0, 12, to_far), one(far, 1, 13, to_near)]

        return first, second, relay

    def open_x(run):
        first, second, _ = gather_x(run)
        start(first() + second())

    def relay_x(run):
        first, _, relay = gather_x(run)
        for c, onward in zip(first(), relay()):
            c.wait_recv()
            onward.start()

    def close_x(run):
        first, second, relay = gather_x(run)
        rest = second() + relay()
        for c in rest:
            c.wait_recv()
        for c in first() + rest:
            c.wait_send()

    def start(copies):
        for c in copies:
            c.start()

    def wait(copies):
        for c in copies:
            c.wait()

    barrier = pltpu.get_barrier_semaphore()
    for peer in [to_y, to_near, to_far] + to_z:
        pl.semaphore_signal(barrier, inc=1, device_id={"dp": peer}, device_id_type=MESH)
    for mate in mates:
        pl.semaphore_signal(barrier, inc=1, device_id={"mp": mate}, device_id_type=MESH)
    load_x = pltpu.make_async_copy(x_hbm, x_ref, lsem.at[0])
    load_up = pltpu.make_async_copy(up_hbm, up_ref, lsem.at[1])
    load_rows = [
        pltpu.make_async_copy(ref, shard.at[f], lsem.at[2 + f])
        for f, ref in enumerate((first_hbm, second_hbm))
    ]
    start(load_rows)
    load_x.start()
    load_up.start()
    wait(load_rows)
    for f in range(2):
        rows = [shard[f, b].astype(F32) for b in range(LOC)]
        rows = jnp.concatenate(rows, axis=0)
        if f == 1:
            buf_b[x, z, h] = rows.astype(BF)
        else:
            low, high = rows[:, :128], rows[:, 128:]
            buf_a[0, x, z, h] = jnp.where(yl < NY // 2, high, low).astype(BF)
            buf_a[1, x, z, h] = jnp.where(yl < NY // 2, low, high).astype(BF)
    pl.semaphore_wait(barrier, 3 + len(to_z) + len(mates))
    own, other, late, second_run = runs
    gather_h(0).start()
    start(gather_z(own))
    for f in range(1, 3):
        gather_h(f).start()
    write_perm(p_x, natural_of_sorted)
    for f in range(3):
        gather_h(f).wait()
        start(gather_z(runs[f + 1]))
    write_perm(p_send, natural_of_send)
    wait(gather_z(own))
    open_x(own)
    write_perm(p_nat, natural_of_gathered)
    relay_x(own)
    wait(gather_z(other))
    open_x(other)
    wait(gather_z(late))
    relay_x(other)
    open_x(late)
    write_perm(p_sort, arrived_of_sorted)
    load_x.wait()
    close_x(own)
    close_x(other)

    def side_lanes(p):
        return pl.ds(pl.multiple_of(sides[p] * 128, 128), 128)

    def sort_first(p):
        rows = buf_a[p].reshape(FEAT, 128)
        for b in range(LOC):
            w1[b, :, side_lanes(p)] = nn(p_nat[b * BLK : (b + 1) * BLK, :], rows).astype(BF)

    def chunk(c):
        return pl.ds(pl.multiple_of(c * tc, tc), tc)

    def block(b):
        return slice(b * BLK, (b + 1) * BLK)

    def launch(send, recv, sems, c, ks):
        for k in ks:
            swap(send.at[c, mates[k]], recv.at[c, mp], sems, c, k).start()

    def launch_all(send, recv, sems, c):
        launch(send, recv, sems, c, range(NM - 1))
        recv[c, mp] = send[c, mp]

    def collect(recv, send, sems, c):
        for k in range(NM - 1):
            swap(send.at[c, mates[k]], recv.at[c, mates[k]], sems, c, k).wait_recv()
        return jnp.concatenate([recv[c, n] for n in range(NM)], axis=1)

    def send_side(half, side, c):
        lanes = nn(half, p_send[...]).astype(BF)
        for n in range(NM // 2):
            send_a[c, side * (NM // 2) + n] = lanes[:, n * 128 : (n + 1) * 128]

    for p in range(2):
        if p == 1:
            relay_x(late)
            wait(gather_z(second_run))
            open_x(second_run)
            close_x(late)
        sort_first(p)
        at = chunk(0)
        half = [nn(x_ref[at, block(b)], w1[b, :, side_lanes(p)]).astype(BF) for b in range(LOC)]
        send_side(jnp.concatenate(half, axis=1), sides[p], 0)
        launch(send_a, recv_a, sem_a, 0, (range(4), range(4, NM - 1))[p])
    recv_a[0, mp] = send_a[0, mp]

    def sort_tokens(at):
        for b in range(LOC):
            xs[at, block(b)] = nn(x_ref[at, block(b)], p_x[...]).astype(BF)

    @pl.loop(1, CHUNKS)
    def _(c):
        at = chunk(c)
        for b in range(LOC):
            u_tmp[:, block(b)] = nn(x_ref[at, block(b)], w1[b]).astype(BF)
        for side in range(2):
            half = [u_tmp[:, b * BLK + side * 128 : b * BLK + side * 128 + 128] for b in range(LOC)]
            send_side(jnp.concatenate(half, axis=1), side, c)
        launch_all(send_a, recv_a, sem_a, c)

        @pl.when(c == 1)
        def _():
            relay_x(second_run)

        sort_tokens(at)

    sort_tokens(chunk(0))
    close_x(second_run)
    write_perm(p_srt, sorted_of_gathered)
    g[...] = jnp.zeros_like(g)
    rows = buf_b[...].reshape(FEAT, BLK)
    for b in range(LOC):
        w2[b] = nn(p_srt[block(b), :], rows).astype(BF)
    load_up.wait()

    @pl.loop(0, CHUNKS)
    def _(c):
        at = chunk(c)
        arrived = collect(recv_a, send_a, sem_a, c)
        for j in range(LOC):
            v = nn(arrived, p_sort[:, block(j)]).astype(BF)
            y = nn(v, w2[j])
            cdf = 0.5 * (1.0 + lax.erf(y * math.sqrt(0.5)))
            mixed_ref[at, block(j)] = (x_ref[at, block(j)].astype(F32) + y * cdf).astype(BF)
            slope = cdf + y * (jnp.exp(-0.5 * y * y) * (1.0 / math.sqrt(2.0 * math.pi)))
            cot = (up_ref[at, block(j)].astype(F32) * slope).astype(BF)
            g[1, j] += tn(v, cot).reshape(NX, 2, 32, BLK)
            u_tmp[:, block(j)] = nt(cot, w2[j]).astype(BF)
        for k in range(LOC):
            lanes = nt(u_tmp[...], p_sort[block(k), :]).astype(BF)
            send_b[c, 2 * k] = lanes[:, :128]
            send_b[c, 2 * k + 1] = lanes[:, 128:]
        launch_all(send_b, recv_b, sem_b, c)

    peer = (to_near, to_far)

    def sum_x1(k):
        return push(s1.at[k], r1.at[k], rsem, k, peer[k])

    def sum_x2(k):
        return push(s2.at[k], r2.at[k], rsem, 2 + k, peer[1 - k])

    def sum_z():
        return [push(s3.at[(z + k) % NZ], r3.at[k - 1], rsem, 3 + k, to_z[k - 1]) for k in range(1, NZ)]

    def sum_h():
        return push(s4, r4, rsem, 11, to_y)

    def reduce_x1():
        for k in range(2):
            s1[k, 0] = g[1, :, (near, far)[k], k].astype(BF)
            s1[k, 1] = g[1, :, opp, k].astype(BF)
            sum_x1(k).start()

    def reduce_x2():
        for k in range(2):
            sum_x1(k).wait_recv()
            s2[k] = (g[1, :, (far, near)[k], k] + r1[k, 1].astype(F32)).astype(BF)
            sum_x2(k).start()

    def reduce_z():
        for k in range(2):
            sum_x2(k).wait_recv()
            part = g[1, :, x, k] + r1[k, 0].astype(F32) + r2[k].astype(F32)
            t[:, k * HALF : (k + 1) * HALF] = part.reshape(LOC, HALF, NH * ROWS, BLK)
        for k in range(NZ):
            s3[k] = t[:, k].reshape(LOC * NH * ROWS, BLK).astype(BF)
        start(sum_z())

    def reduce_h():
        total = t[:, z].reshape(LOC * NH * ROWS, BLK)
        copies = sum_z()
        for k in range(NZ - 1):
            copies[k].wait_recv()
            total = total + r3[k].astype(F32)
        total = total.reshape(LOC, NH * ROWS, BLK)
        s4[...] = jnp.where(h == 0, total[:, ROWS:], total[:, :ROWS])
        gsecond_ref[...] = jnp.where(h == 0, total[:, :ROWS], total[:, ROWS:])
        sum_h().start()

    def reduce_end():
        sum_h().wait_recv()
        gsecond_ref[...] = (gsecond_ref[...] + r4[...]) * scale
        for k in range(2):
            sum_x1(k).wait_send()
            sum_x2(k).wait_send()
        for c in sum_z():
            c.wait_send()
        sum_h().wait_send()

    def rows_copy(src, dst, sems, out_slot, in_slot, to):
        return pltpu.make_async_remote_copy(
            src_ref=src, dst_ref=dst, send_sem=sems.at[0, out_slot], recv_sem=sems.at[1, in_slot],
            device_id={"dp": to}, device_id_type=MESH,
        )

    def cross_x(to, slot):
        return rows_copy(s5.at[0, to], rx.at[slot], xsem, to, slot, dp_of(z, h, to))

    def cross_z(to, slot):
        return rows_copy(s6.at[to], r6.at[slot], zsem, to, slot, dp_of(to, 1 - h, x))

    def same(to, slot):
        return rows_copy(
            s5.at[1, to // NZ, to % NZ], r5.at[slot], fsem, to, slot, dp_of(to % NZ, h, to // NZ)
        )

    spot = x * NZ + z

    def send_final(side, hh):
        low = lax.broadcasted_iota(jnp.int32, (NZ, NH * ROWS, BLK), 1) < ROWS
        for xx in range(NX):
            pair = []
            for b in (0, 2):
                one, two = (g[0, b + k, xx].reshape(NZ, NH * ROWS, BLK) for k in range(2))
                if hh == 0:
                    pair.append(jnp.where(low, one, pltpu.roll(two, ROWS, 1)))
                else:
                    pair.append(jnp.where(low, pltpu.roll(one, ROWS, 1), two))
            s5[side, xx] = jnp.concatenate(pair, axis=1).astype(BF)
            if side == 0:
                pl.when(x != xx)(lambda: cross_x(xx, x).start())
            else:

                @pl.loop(xx * NZ, (xx + 1) * NZ)
                def _(to):
                    pl.when(to != spot)(lambda: same(to, spot).start())

    def cross_final():
        acc = s5[0, x].astype(F32)
        for k in (near, far, opp):
            cross_x(k, k).wait_recv()
            acc = acc + rx[k].astype(F32)
        s6[...] = acc.astype(BF)

        @pl.loop(0, NZ)
        def _(to):
            cross_z(to, z).start()

    reduce_x1()

    def first_grad(c):
        at = chunk(c)
        arrived = collect(recv_b, send_b, sem_b, c)
        side = [nt(arrived[:, k * 512 : (k + 1) * 512], p_send[...]).astype(BF) for k in range(2)]
        for b in range(LOC):
            du = jnp.concatenate([v[:, b * 128 : (b + 1) * 128] for v in side], axis=1)
            u_tmp[:, block(b)] = du
            g[0, b] += tn(xs[at, block(b)], du).reshape(NX, 2, 32, BLK)

    def token_grad(c):
        at = chunk(c)
        for b in range(LOC):
            back = nt(u_tmp[:, block(b)], w1[b])
            gtok_ref[at, block(b)] = (up_ref[at, block(b)].astype(F32) + back).astype(BF)

    @pl.loop(0, CHUNKS - 1)
    def _(c):
        first_grad(c)
        token_grad(c)
        for step, run in enumerate((reduce_x2, reduce_z, reduce_h)):
            pl.when(c == step)(run)

    first_grad(CHUNKS - 1)
    for hh in range(NH):

        @pl.when(h == hh)
        def _():
            send_final(0, 1 - hh)
            send_final(1, hh)

    token_grad(CHUNKS - 1)
    cross_final()
    reduce_end()

    @pl.loop(0, CHUNKS)
    def _(c):
        for k in range(NM - 1):
            swap(send_a.at[c, mates[k]], recv_a.at[c, mp], sem_a, c, k).wait_send()
            swap(send_b.at[c, mates[k]], recv_b.at[c, mp], sem_b, c, k).wait_send()

    def add_same(i, total):
        peer = (spot + i) % (NX * NZ)
        same(peer, peer).wait_recv()
        return total + r5[peer].astype(F32)

    def add_cross(i, total):
        cross_z(i, i).wait_recv()
        return total + r6[i].astype(F32)

    total = lax.fori_loop(1, NX * NZ, add_same, s5[1, x, z].astype(F32))
    total = lax.fori_loop(0, NZ, add_cross, total) * scale
    for b in range(LOC):
        gfirst_ref[b] = total[b * ROWS : (b + 1) * ROWS]

    for k in (near, far, opp):
        cross_x(k, k).wait_send()

    @pl.loop(0, NZ)
    def _(i):
        cross_z(i, i).wait_send()

    @pl.loop(1, NX * NZ)
    def _(i):
        peer = (spot + i) % (NX * NZ)
        same(peer, peer).wait_send()


def store_kernel(*refs):
    count = len(refs) // 2
    sems = refs[-1]
    copies = [
        pltpu.make_async_copy(refs[i], refs[count + i], sems.at[i]) for i in range(count)
    ]
    for c in copies:
        c.start()
    for c in copies:
        c.wait()


def store(results):
    count = len(results)
    return pl.pallas_call(
        store_kernel,
        out_shape=tuple(jax.ShapeDtypeStruct(r.shape, r.dtype) for r in results),
        in_specs=[pl.BlockSpec(memory_space=pltpu.VMEM)] * count,
        out_specs=(pl.BlockSpec(memory_space=pltpu.HBM),) * count,
        scratch_shapes=[pltpu.SemaphoreType.DMA((count,))],
        name="store_results",
    )(*(pltpu.with_memory_space_constraint(r, pltpu.VMEM) for r in results))


def on_device(*args):
    tok = args[0].shape[0]
    tc = tok // CHUNKS
    scale = 1.0 / math.sqrt(tok * lax.axis_size("dp"))
    vmem = pl.BlockSpec(memory_space=pltpu.VMEM)
    hbm = pl.BlockSpec(memory_space=pltpu.HBM)
    dma = pltpu.SemaphoreType.DMA
    slot = NH * ROWS
    results = pl.pallas_call(
        functools.partial(kernel, scale),
        out_shape=(
            jax.ShapeDtypeStruct((tok, FEAT), BF),
            jax.ShapeDtypeStruct((tok, FEAT), BF),
            jax.ShapeDtypeStruct((LOC, ROWS, BLK), F32),
            jax.ShapeDtypeStruct((LOC, ROWS, BLK), F32),
        ),
        in_specs=[hbm] * 4,
        out_specs=(vmem,) * 4,
        scratch_shapes=[
            pltpu.VMEM((tok, FEAT), BF),
            pltpu.VMEM((tok, FEAT), BF),
            pltpu.VMEM((2, LOC, ROWS, BLK), BF),
            pltpu.VMEM((2, NX, NZ, NH, LOC * ROWS, 128), BF),
            pltpu.VMEM((NX, NZ, NH, LOC * ROWS, BLK), BF),
            pltpu.VMEM((LOC, BLK, BLK), BF),
            pltpu.VMEM((LOC, BLK, BLK), BF),
            pltpu.VMEM((tok, FEAT), BF),
            pltpu.VMEM((FEAT // 2, FEAT // 2), BF),
            pltpu.VMEM((FEAT, FEAT), BF),
            pltpu.VMEM((FEAT, FEAT), BF),
            pltpu.VMEM((FEAT, FEAT), BF),
            pltpu.VMEM((BLK, BLK), BF),
            pltpu.VMEM((tc, FEAT), BF),
            pltpu.VMEM((CHUNKS, NM, tc, 128), BF),
            pltpu.VMEM((CHUNKS, NM, tc, 128), BF),
            pltpu.VMEM((CHUNKS, NM, tc, 128), BF),
            pltpu.VMEM((CHUNKS, NM, tc, 128), BF),
            pltpu.VMEM((2, LOC, NX, 2, HALF * slot, BLK), F32),
            pltpu.VMEM((2, 2, LOC, HALF * slot, BLK), BF),
            pltpu.VMEM((2, 2, LOC, HALF * slot, BLK), BF),
            pltpu.VMEM((2, LOC, HALF * slot, BLK), BF),
            pltpu.VMEM((2, LOC, HALF * slot, BLK), BF),
            pltpu.VMEM((LOC, NZ, slot, BLK), F32),
            pltpu.VMEM((NZ, LOC * slot, BLK), BF),
            pltpu.VMEM((NZ - 1, LOC * slot, BLK), BF),
            pltpu.VMEM((LOC, ROWS, BLK), F32),
            pltpu.VMEM((LOC, ROWS, BLK), F32),
            pltpu.VMEM((2, NX, NZ, LOC * ROWS, BLK), BF),
            pltpu.VMEM((NX, NZ, LOC * ROWS, BLK), BF),
            pltpu.VMEM((NZ, LOC * ROWS, BLK), BF),
            pltpu.VMEM((NZ, LOC * ROWS, BLK), BF),
            pltpu.VMEM((NX * NZ, LOC * ROWS, BLK), BF),
            dma((4,)),
            dma((3, 2, 28)),
            dma((2, CHUNKS, NM - 1)),
            dma((2, CHUNKS, NM - 1)),
            dma((2, 12)),
            dma((2, NX * NZ)),
            dma((2, NX)),
            dma((2, NZ)),
        ],
        compiler_params=pltpu.CompilerParams(
            collective_id=0, has_side_effects=True, vmem_limit_bytes=40 * 1024 * 1024
        ),
        name="monarch_layer",
    )(*(pltpu.with_memory_space_constraint(v, pltpu.HBM) for v in args))
    return store(results)


def solution(mesh):
    placed = (P("dp", "mp"), P("dp", "mp"), P("mp", "dp", None), P("mp", "dp", None))
    return jax.shard_map(
        on_device, mesh=mesh, in_specs=placed, out_specs=placed, check_vma=False
    )
```
